128 devices in a mesh: px: 8 (over x, core), py: 16 (over y, z).
Axes of the slice: x: 4, y: 4, z: 4, core: 2. Of those that a mesh axis runs over, the one named last changes fastest.
Arguments:
- cell_ids: int32 [131072, 128], P(('px', 'py')), may hold values from 0 to 32767
- masses: bfloat16 [131072, 128], P(('px', 'py')), may hold values from 0.5 to 2
- block_dest: int32 [131072, 1], P(('px', 'py')), may hold values from 0 to 1023; in each aligned block of 1024 rows (0 to 1023, 1024 to 2047, ...) at most 2 rows name the same one
- block_count: int32 [131072], P(('px', 'py')), may hold values from 1 to 128
- screen: float32 [8], replicated, may hold values from 0.02 to 0.2
Outputs:
- potential_modes: float32 [8, 128, 256], P(None, None, ('px', 'py'))
The draws below stay inside these ranges and needn't reach their ends.
Inputs may be any that keep to these rules, and one draw needn't show every extreme that they name: `block_dest`: tile t lies on device t // 8 (devices numbered px-major) and plane t % 8. Among the 1024 blocks of one device no tile is named more than 2 times, a bound that some block reaches. `block_count`: the live particles of a block are its first ones. `cell_ids`: A cell c is row c // 128 and column c % (128) of the tile.
All inputs are finite; a program needn't handle non-finite values.
Results may differ from the reference program's by a relative error of at most 0.0003.
Values may be sent and summed in bfloat16 or wider, within the bound.
A program may use at most 64 MiB of HBM per device.

```python
import math
import jax
import jax.numpy as jnp
import numpy as np
from jax import lax

NY = 2048
NZ = 2048
PL = 8
KY = 128
KZ = 128
CAP = 2
NB = 1024
BS = 128
BLOCKS = 131072
TILES = 1024
N_PX = 8
N_PY = 16


def with_ends(array, rng, smallest, top_value):
    longest = array.shape.index(max(array.shape))
    spots = []
    for shift in (0, 1):
        where = [jax.random.randint(jax.random.fold_in(rng, axis), (), 0, length) for axis, length in enumerate(array.shape)]
        where[longest] = (where[longest] + shift) % array.shape[longest]
        spots.append(tuple(where))
    return array.at[spots[0]].set(smallest).at[spots[1]].set(top_value)


def level_of(stream_key, shape, shards, smallest, top_value):
    level, own = 1.0, jax.random.fold_in(stream_key, 6)
    for dim, parts in shards:
        steps = jnp.exp(jax.random.uniform(jax.random.fold_in(own, dim), (parts,), jnp.float32, smallest / len(shards), top_value / len(shards)))
        level = level * jnp.repeat(steps, shape[dim] // parts).reshape([-1 if axis == dim else 1 for axis in range(len(shape))])
    return level


def assign_block(key, own, number, rows, amount, top, bound, skew):
    sequence = jax.random.permutation(key, amount)
    crowded, common = portions_of(amount, rows * top, bound, skew, True), portions_of(amount, rows * top, bound, skew, False)
    places = jnp.arange(amount)

    def named(lengths, offset_by):
        used = int((lengths > 0).sum())
        fixed = max(1, used // 4)
        moved = fixed + (places - fixed + offset_by * (used - fixed)) % max(1, amount - fixed)
        return jnp.zeros((amount,), jnp.int32).at[sequence[jnp.where(places < fixed, places, moved)]].set(jnp.asarray(lengths, jnp.int32))

    lengths = jnp.where(number % 4 == 0, named(crowded, number // 4), named(common, number - number // 4 - 1))
    mixed = jax.random.permutation(jax.random.fold_in(own, 3), amount)
    source_of, taker = mixed[0:amount // 2 * 2:2], mixed[1:amount // 2 * 2:2]
    room = jnp.minimum(lengths[source_of] - 1, bound - lengths[taker]) // 2
    room = jnp.where((source_of == sequence[0]) | (taker == sequence[0]) | (lengths[taker] == 0), 0, jnp.maximum(room, 0))
    moved = jax.random.randint(jax.random.fold_in(own, 4), (amount // 2,), 0, 1 << 20) % (room + 1)
    lengths = lengths.at[source_of].add(-moved).at[taker].add(moved)
    items = jnp.searchsorted(jnp.cumsum(lengths), jnp.arange(rows * top), side="right").astype(jnp.int32)
    grid = items.reshape(top, rows).T
    grid = grid[jax.random.permutation(jax.random.fold_in(own, 1), rows)]
    offset_by = jax.random.randint(jax.random.fold_in(own, 2), (rows, 1), 0, top)
    return jnp.take_along_axis(grid, (jnp.arange(top)[None, :] + offset_by) % top, axis=1)


def portions_of(number_of, total, most, lean, full):
    loads = [(1 << 20) // math.isqrt(standing ** lean) + 1 for standing in range(1, number_of + 1)]
    largest = most if full else min(most, max(-(-total // number_of), total * loads[0] // sum(loads)))
    least = 1 if total - largest >= number_of - 1 else 0
    holding, spare = [largest] + [least] * (number_of - 1), total - largest - least * (number_of - 1)
    while spare > 0:
        movable = [i for i in range(1, number_of) if holding[i] < largest] or [i for i in range(1, number_of) if holding[i] < most]
        whole, budget = sum([loads[i] for i in movable]), spare
        for i in movable:
            more = min(most - holding[i], max(1, budget * loads[i] // whole), spare)
            holding[i] = holding[i] + more
            spare = spare - more
    return np.array(holding)


def setup_inputs(seed: int = 0) -> dict:
    streams_of = jax.random.split(jax.random.key(seed), 6)
    cell_ids = with_ends(jax.random.randint(streams_of[0], (BLOCKS, BS), 0, (NY // N_PX) * (NZ // N_PY)), jax.random.fold_in(streams_of[0], 1), 0, ((NY // N_PX) * (NZ // N_PY)) - 1).astype(jnp.int32)
    masses = jnp.clip(jnp.exp(math.log(2.0) - 1.3862944 * jax.random.uniform(streams_of[1], (BLOCKS, BS), jnp.float32) ** level_of(streams_of[1], (BLOCKS, BS), ((0, 128),), -0.2, 0.2)), 0.5, 2.0).astype(jnp.bfloat16)
    block_dest_keys = jax.random.split(jax.random.fold_in(streams_of[2], 1), BLOCKS // NB)
    block_dest_turns = jax.random.permutation(jax.random.fold_in(streams_of[2], 3), BLOCKS // NB)
    block_dest = jax.vmap(lambda own, number: assign_block(jax.random.fold_in(streams_of[2], 2), own, number, NB, TILES, 1, CAP, 2))(block_dest_keys, block_dest_turns).reshape((BLOCKS, 1))
    block_count = with_ends(jax.random.randint(streams_of[3], (BLOCKS,), 1, BS + 1), jax.random.fold_in(streams_of[3], 1), 1, BS).astype(jnp.int32)
    screen = jnp.clip(jnp.exp(jax.random.uniform(streams_of[4], (PL,), jnp.float32, math.log(0.02), math.log(0.2))), 0.02, 0.2)
    return {"cell_ids": cell_ids, "masses": masses, "block_dest": block_dest, "block_count": block_count, "screen": screen}


def green_table(screen):
    y_freq = (jnp.arange(KY) - KY // 2).astype(jnp.float32)[:, None]
    z_freq = (jnp.arange(KZ) - KZ // 2).astype(jnp.float32)[None, :]
    wave_sq = (2.0 * jnp.sin(math.pi * y_freq / NY)) ** 2 + (2.0 * jnp.sin(math.pi * z_freq / NZ)) ** 2
    is_zero = (y_freq == 0.0) & (z_freq == 0.0)
    scr = screen[:, None, None]
    return jnp.where(is_zero[None], jnp.zeros_like(wave_sq)[None], -scr / (wave_sq[None] + scr))

def reference(cell_ids, masses, block_dest, block_count, screen):
    tile_rows = NY // N_PX
    tile_cols = NZ // N_PY
    places = lax.broadcasted_iota(jnp.int32, cell_ids.shape, 1)
    weight = jnp.where(places < block_count[:, None], masses, jnp.zeros_like(masses)).astype(jnp.float32)
    dest_tile = block_dest[:, 0]
    owner_dev = dest_tile // PL
    plane_of = dest_tile % PL
    row_base = owner_dev // N_PY * tile_rows
    col_base = owner_dev % N_PY * tile_cols
    rows_all = (row_base[:, None] + cell_ids // tile_cols).reshape(-1).astype(jnp.int32)
    cols_all = (col_base[:, None] + cell_ids % tile_cols).reshape(-1).astype(jnp.int32)
    planes_all = jnp.broadcast_to(plane_of[:, None], cell_ids.shape).reshape(-1).astype(jnp.int32)
    density = jnp.zeros((PL, NY, NZ), jnp.float32).at[planes_all, rows_all, cols_all].add(weight.reshape(-1))
    z_modes = ((jnp.arange(KZ) - KZ // 2) % NZ).astype(jnp.int32)
    y_modes = ((jnp.arange(KY) - KY // 2) % NY).astype(jnp.int32)
    along_z = jnp.fft.fft(density, axis=2)[:, :, z_modes]
    spectrum = jnp.fft.fft(along_z, axis=1)[:, y_modes, :]
    green_fn = green_table(screen)
    scale = 1.0 / math.sqrt(NY * NZ)
    real_part = jnp.real(spectrum) * green_fn * scale
    imag_part = jnp.imag(spectrum) * green_fn * scale
    return jnp.stack([real_part, imag_part], axis=-1).reshape(PL, KY, 2 * KZ)
```

```python
import math

import jax
import jax.numpy as jnp
import numpy as np
from jax import lax
from jax.experimental import pallas as pl
from jax.experimental.pallas import tpu as pltpu
from jax.sharding import PartitionSpec as P

NY = 2048
NZ = 2048
PL = 8
KY = 128
KZ = 128
N_PY = 16
SUB = 128
Q = 32
UNROLL = 16


def polynomial_table():
    x = (np.arange(SUB) - (SUB - 1) / 2) / (SUB / 2)
    return np.cos(np.arange(Q)[:, None] * np.arccos(x)[None, :])


def twiddle_factors(length):
    freqs = np.arange(128) - 64
    angle = 2.0 * np.pi * freqs / length
    nodes = (np.arange(512) + 0.5) * np.pi / 512
    waves = np.exp(-1j * (angle * SUB / 2)[:, None] * np.cos(nodes)[None, :])
    coefs = (2.0 / 512) * waves @ np.cos(nodes[:, None] * np.arange(Q)[None, :])
    coefs[:, 0] /= 2
    starts = np.arange(length // SUB) * SUB + (SUB - 1) / 2
    shift = np.exp(-1j * starts[:, None] * angle[None, :])
    return shift[:, None, :] * coefs.T[None, :, :]


def block_kernel(dest_ref, count_ref, table_ref, cells_ref, mass_ref, out_ref):
    out_ref[...] = jnp.zeros_like(out_ref)
    lane = lax.broadcasted_iota(jnp.int32, (1, SUB), 1)

    def step(group, carry):
        base = pl.multiple_of(group * UNROLL, UNROLL)
        cells = cells_ref[pl.ds(base, UNROLL), :]
        mass = mass_ref[pl.ds(base, UNROLL), :].astype(jnp.float32)
        table = table_ref[...]
        for j in range(UNROLL):
            tile = dest_ref[base + j]
            count = count_ref[base + j]
            plane = tile % PL
            device = tile // PL
            tile_row = device // N_PY
            tile_col = device % N_PY
            cell = cells[j : j + 1, :]
            w = jnp.where(lane < count, mass[j : j + 1, :], 0.0)
            z_at = jnp.broadcast_to(cell & (SUB - 1), (Q, SUB))
            y_at = jnp.broadcast_to((cell >> 7) & (SUB - 1), (Q, SUB))
            quarter = (cell >> 14) + 2 * (tile_row % 2)
            z = jnp.take_along_axis(table, z_at, axis=1) * w
            y = jnp.take_along_axis(table, y_at, axis=1)
            z_hi = z.astype(jnp.bfloat16)
            z_lo = (z - z_hi.astype(jnp.float32)).astype(jnp.bfloat16)
            y_hi = y.astype(jnp.bfloat16)
            y_lo = (y - y_hi.astype(jnp.float32)).astype(jnp.bfloat16)
            picks = [(quarter == k).astype(jnp.float32).astype(jnp.bfloat16) for k in range(4)]
            y_hi = jnp.concatenate([y_hi * pick for pick in picks], axis=0)
            y_lo = jnp.concatenate([y_lo * pick for pick in picks], axis=0)
            left = jnp.concatenate([z_hi, z_hi, z_lo], axis=1)
            right = jnp.concatenate([y_hi, y_lo, y_hi], axis=1)
            part = lax.dot_general(
                left, right, (((1,), (1,)), ((), ())), preferred_element_type=jnp.float32
            )
            row = pl.multiple_of((plane * N_PY + tile_col) * Q, Q)
            out_ref[tile_row // 2, pl.ds(row, Q), :] += part
        return carry

    lax.fori_loop(0, cells_ref.shape[0] // UNROLL, step, 0)


def block_sums(dest, count, table, cells, mass):
    rows = PL * N_PY * Q
    return pl.pallas_call(
        block_kernel,
        out_shape=jax.ShapeDtypeStruct((4, rows, SUB), jnp.float32),
        in_specs=[pl.BlockSpec(memory_space=pltpu.SMEM)] * 2
        + [pl.BlockSpec(memory_space=pltpu.VMEM)] * 3,
        out_specs=pl.BlockSpec(memory_space=pltpu.VMEM),
        compiler_params=pltpu.CompilerParams(vmem_limit_bytes=48 << 20),
    )(dest, count, table, cells, mass)


def shards(cell_ids, masses, block_dest, block_count, screen):
    table = jnp.asarray(polynomial_table(), jnp.float32)
    sums = block_sums(block_dest[:, 0], block_count, table, cell_ids, masses)
    grid = sums.reshape(4, PL, N_PY * Q, SUB)
    z_factors = twiddle_factors(NZ).reshape(N_PY * Q, KZ)
    y_factors = twiddle_factors(NY).reshape(4, SUB, KY)
    z_side = jnp.asarray(np.stack([z_factors.real, z_factors.imag]), jnp.float32)
    y_cos = jnp.asarray(np.stack([y_factors.real, y_factors.imag]), jnp.float32)
    y_sin = jnp.asarray(np.stack([-y_factors.imag, y_factors.real]), jnp.float32)
    exact = lax.Precision.HIGHEST
    half = jnp.einsum("czn,ipzl->cpnil", z_side, grid, precision=exact)
    partial = jnp.einsum("pnil,cilm->npcm", half[0], y_cos, precision=exact)
    partial += jnp.einsum("pnil,cilm->npcm", half[1], y_sin, precision=exact)
    total = lax.psum_scatter(partial, ("px", "py"), scatter_dimension=0, tiled=True)[0]
    device = lax.axis_index("px") * lax.axis_size("py") + lax.axis_index("py")
    z_freq = (device - KZ // 2).astype(jnp.float32)
    y_freq = (lax.broadcasted_iota(jnp.int32, (1, KY), 1) - KY // 2).astype(jnp.float32)
    wave_sq = (2.0 * jnp.sin(math.pi * y_freq / NY)) ** 2 + (
        2.0 * jnp.sin(math.pi * z_freq / NZ)
    ) ** 2
    scr = screen[:, None]
    green = jnp.where((y_freq == 0.0) & (z_freq == 0.0), 0.0, -scr / (wave_sq + scr))
    modes = total * green[:, None, :] * (1.0 / math.sqrt(NY * NZ))
    return jnp.swapaxes(modes, 1, 2)


def solution(mesh):
    return jax.shard_map(
        shards,
        mesh=mesh,
        in_specs=(
            P(("px", "py"), None),
            P(("px", "py"), None),
            P(("px", "py"), None),
            P(("px", "py")),
            P(),
        ),
        out_specs=P(None, None, ("px", "py")),
        check_vma=False,
    )
```

```python
import math

import jax
import jax.numpy as jnp
import ml_dtypes
import numpy as np
from jax import lax
from jax.experimental import pallas as pl
from jax.experimental.pallas import tpu as pltpu
from jax.sharding import PartitionSpec as P

NY = 2048
NZ = 2048
PL = 8
KY = 128
KZ = 128
N_PX = 8
N_PY = 16
DEVICES = N_PX * N_PY
SUB = 128
Q = 32
UNROLL = 64
SPAN = N_PY * Q
HALF = 72
PARTS = 2 * PL
SLOTS = 129

MESH = pl.DeviceIdType.MESH


def twiddle_factors(freqs, length):
    angle = 2.0 * np.pi * freqs / length
    nodes = (np.arange(512) + 0.5) * np.pi / 512
    waves = np.exp(-1j * (angle * SUB / 2)[:, None] * np.cos(nodes)[None, :])
    coefs = (2.0 / 512) * waves @ np.cos(nodes[:, None] * np.arange(Q)[None, :])
    coefs[:, 0] /= 2
    starts = np.arange(length // SUB) * SUB + (SUB - 1) / 2
    shift = np.exp(-1j * starts[:, None] * angle[None, :])
    return (shift[:, None, :] * coefs.T[None, :, :]).reshape(-1, len(freqs))


def two_parts(values):
    high = values.astype(ml_dtypes.bfloat16)
    low = (values - high.astype(np.float64)).astype(ml_dtypes.bfloat16)
    return high, low


def z_table():
    factors = twiddle_factors(np.arange(HALF) * (np.arange(HALF) <= 64), NZ)
    return np.concatenate(two_parts(np.concatenate([factors.real, factors.imag], axis=1).T))


def y_table():
    factors = twiddle_factors(np.arange(KY) - KY // 2, NY)
    real, imag = factors.real, factors.imag
    both = np.stack(
        [np.concatenate([real, imag], axis=1), np.concatenate([-imag, real], axis=1)]
    )
    return np.stack(two_parts(both))


def split(values):
    high = values.astype(jnp.bfloat16)
    return high, (values - high.astype(jnp.float32)).astype(jnp.bfloat16)


def dot(a, b):
    return jnp.dot(a, b, preferred_element_type=jnp.float32)


def chain(ref, first, x):
    twice = x + x
    before, now = first, first * x
    ref[0:8, :] = before
    ref[8:16, :] = now
    for q in range(2, Q):
        before, now = now, twice * now - before
        ref[8 * q : 8 * q + 8, :] = now


def block_kernel(dest_ref, count_ref, cells_ref, mass_ref, z_ref, y_ref, out_ref, sums, half, *chains):
    sums[...] = jnp.zeros_like(sums)
    lane = lax.broadcasted_iota(jnp.int32, (8, SUB), 1)
    upper = lax.broadcasted_iota(jnp.int32, (Q, SUB), 1) >= SUB // 2

    def step(group, carry):
        none = jnp.zeros((Q, SUB), jnp.bfloat16)
        first = pl.multiple_of(group * UNROLL, UNROLL)
        masses = mass_ref[pl.ds(first, UNROLL), :].astype(jnp.float32)
        for eight in range(UNROLL // 8):
            z_chain, y_chain = chains[2 * eight], chains[2 * eight + 1]
            base = pl.multiple_of(first + 8 * eight, 8)
            cells = cells_ref[pl.ds(base, 8), :]
            live = lane < count_ref[pl.ds(base, 8), :]
            weight = jnp.where(live, masses[8 * eight : 8 * eight + 8], 0.0)
            z_at = ((cells & (SUB - 1)).astype(jnp.float32) - (SUB - 1) / 2) * (2 / SUB)
            y_at = (((cells >> 7) & (SUB - 1)).astype(jnp.float32) - (SUB - 1) / 2) * (2 / SUB)
            chain(z_chain, weight, z_at)
            chain(y_chain, jnp.ones_like(weight), y_at)
            lower_half = (cells >> 14).astype(jnp.float32)
            for pair in range(0, 8, 2):
                left, right = [], []
                for j in (pair, pair + 1):
                    rows = [pl.ds(64 * i + j, 8, stride=8) for i in range(Q // 8)]
                    left.append(split(jnp.concatenate([z_chain[r, :] for r in rows], axis=0)))
                    high, low = split(jnp.concatenate([y_chain[r, :] for r in rows], axis=0))
                    second = lower_half[j : j + 1]
                    first_half = (1.0 - second).astype(jnp.bfloat16)
                    second = second.astype(jnp.bfloat16)
                    right.append(
                        jnp.concatenate(
                            [high * first_half, high * second, low * first_half, low * second],
                            axis=0,
                        )
                    )
                left = jnp.concatenate(
                    [
                        jnp.concatenate([left[0][0], left[0][1], none, none], axis=0),
                        jnp.concatenate([none, none, left[1][0], left[1][1]], axis=0),
                    ],
                    axis=1,
                )
                part = lax.dot_general(
                    left,
                    jnp.concatenate(right, axis=1),
                    (((1,), (1,)), ((), ())),
                    preferred_element_type=jnp.float32,
                )
                for j in range(2):
                    tile = dest_ref[base + pair + j]
                    plane, device = tile & (PL - 1), tile >> 3
                    tile_row, tile_col = device >> 4, device & (N_PY - 1)
                    block = part[64 * j : 64 * j + 32] + part[64 * j + 32 : 64 * j + 64]
                    block = block + pltpu.roll(block, SUB // 2, 1)
                    block = jnp.where(upper == ((tile_row & 1) == 1), block, 0.0)
                    row = pl.multiple_of((plane * N_PY + tile_col) * Q, Q)
                    sums[tile_row >> 1, pl.ds(row, Q), :] += block
        return carry

    lax.fori_loop(0, cells_ref.shape[0] // UNROLL, step, 0)

    def transform(plane, carry):
        row = pl.multiple_of(plane * SPAN, SPAN)
        for i in range(4):
            high, low = split(sums[i, pl.ds(row, SPAN), :])
            product = dot(z_ref[0 : 2 * HALF, :], jnp.concatenate([high, low], axis=1))
            product = product[:, :SUB] + product[:, SUB:]
            product += dot(z_ref[2 * HALF :, :], high)
            half[:, SUB * i : SUB * i + SUB] = product
        modes = []
        for c in range(2):
            high, low = split(half[HALF * c : HALF * c + HALF, :])
            modes.append(
                dot(high, y_ref[0, c]) + dot(low, y_ref[0, c]) + dot(high, y_ref[1, c])
            )
        plus, minus = modes[0] + modes[1], modes[0] - modes[1]
        for c in range(2):
            lanes = slice(KY * c, KY * c + KY)
            at = PL * c + plane
            out_ref[pl.ds(at, 64, stride=PARTS), :] = plus[0:64, lanes]
            out_ref[pl.ds(64 * PARTS + at, 65, stride=PARTS), :] = minus[0:65, lanes]
        return carry

    lax.fori_loop(0, PL, transform, 0)


def partial_modes(dest, count, cells, mass):
    blocks = cells.shape[0]
    counts = jnp.broadcast_to(count[:, None], (blocks, SUB))
    return pl.pallas_call(
        block_kernel,
        out_shape=jax.ShapeDtypeStruct((SLOTS * PARTS, KY), jnp.float32),
        in_specs=[pl.BlockSpec(memory_space=pltpu.SMEM)]
        + [pl.BlockSpec(memory_space=pltpu.VMEM)] * 5,
        out_specs=pl.BlockSpec(memory_space=pltpu.VMEM),
        scratch_shapes=[
            pltpu.VMEM((4, PL * SPAN, SUB), jnp.float32),
            pltpu.VMEM((2 * HALF, SPAN), jnp.float32),
        ]
        + [pltpu.VMEM((Q * 8, SUB), jnp.float32)] * (UNROLL // 4),
        compiler_params=pltpu.CompilerParams(vmem_limit_bytes=48 << 20),
    )(dest, counts, cells, mass, jnp.asarray(z_table()), jnp.asarray(y_table()))


def position():
    return lax.axis_index("px") * N_PY + lax.axis_index("py")


def slot_of(device):
    ahead = device // 64
    return ahead * (device - 64) + (1 - ahead) * (128 - device)


def exchange_kernel(part_ref, green_ref, out_ref, landed, send_sem, recv_sem):
    me = position()
    barrier = pltpu.get_barrier_semaphore()

    def greet(k, carry):
        to = lax.rem(me + k, DEVICES)
        pl.semaphore_signal(barrier, inc=1, device_id=(to // N_PY, to % N_PY), device_id_type=MESH)
        return carry

    lax.fori_loop(1, DEVICES, greet, 0)
    pl.semaphore_wait(barrier, DEVICES - 1)

    def send(k, carry):
        to = lax.rem(me + k, DEVICES)
        pltpu.make_async_remote_copy(
            src_ref=part_ref.at[pl.ds(pl.multiple_of(slot_of(to) * PARTS, PARTS), PARTS)],
            dst_ref=landed.at[pl.ds(pl.multiple_of((k - 1) * PARTS, PARTS), PARTS)],
            send_sem=send_sem,
            recv_sem=recv_sem,
            device_id=(to // N_PY, to % N_PY),
            device_id_type=MESH,
        ).start()
        return carry

    lax.fori_loop(1, DEVICES, send, 0)
    pltpu.make_async_copy(landed, landed, recv_sem).wait()
    total = part_ref[pl.ds(pl.multiple_of(slot_of(me) * PARTS, PARTS), PARTS), :]
    parts = landed[...].reshape(DEVICES - 1, PARTS, KY)
    out_ref[...] = (total + jnp.sum(parts, axis=0)) * green_ref[...]
    pltpu.make_async_copy(landed, landed, send_sem).wait()


def exchange(part, green):
    return pl.pallas_call(
        exchange_kernel,
        out_shape=jax.ShapeDtypeStruct((PARTS, KY), jnp.float32),
        in_specs=[pl.BlockSpec(memory_space=pltpu.VMEM)] * 2,
        out_specs=pl.BlockSpec(memory_space=pltpu.VMEM),
        scratch_shapes=[
            pltpu.VMEM(((DEVICES - 1) * PARTS, KY), jnp.float32),
            pltpu.SemaphoreType.DMA,
            pltpu.SemaphoreType.DMA,
        ],
        compiler_params=pltpu.CompilerParams(collective_id=0, has_side_effects=True),
    )(part, green)


def shards(cell_ids, masses, block_dest, block_count, screen):
    part = partial_modes(block_dest[:, 0], block_count, cell_ids, masses)
    z_freq = (position() - KZ // 2).astype(jnp.float32)
    y_freq = (lax.broadcasted_iota(jnp.int32, (1, KY), 1) - KY // 2).astype(jnp.float32)
    wave_sq = (2.0 * jnp.sin(math.pi * y_freq / NY)) ** 2 + (
        2.0 * jnp.sin(math.pi * z_freq / NZ)
    ) ** 2
    scr = screen[:, None]
    green = jnp.where((y_freq == 0.0) & (z_freq == 0.0), 0.0, -scr / (wave_sq + scr))
    green = green * (1.0 / math.sqrt(NY * NZ))
    modes = exchange(part, jnp.concatenate([green, green], axis=0))
    return jnp.moveaxis(modes.reshape(2, PL, KY), 0, 2)


def solution(mesh):
    return jax.shard_map(
        shards,
        mesh=mesh,
        in_specs=(
            P(("px", "py"), None),
            P(("px", "py"), None),
            P(("px", "py"), None),
            P(("px", "py")),
            P(),
        ),
        out_specs=P(None, None, ("px", "py")),
        check_vma=False,
    )
```

```python
import math

import jax
import jax.numpy as jnp
import ml_dtypes
import numpy as np
from jax import lax
from jax.experimental import pallas as pl
from jax.experimental.pallas import tpu as pltpu
from jax.sharding import PartitionSpec as P

NY = 2048
NZ = 2048
PL = 8
KY = 128
KZ = 128
N_PX = 8
N_PY = 16
DEVICES = N_PX * N_PY
SUB = 128
Q = 32
UNROLL = 64
SPAN = N_PY * Q
HALF = 72
ROWS = 2 * HALF
HELD = PL // 2
PARTS = 2 * HELD

MESH = pl.DeviceIdType.MESH


def twiddle_factors(freqs, length):
    angle = 2.0 * np.pi * freqs / length
    nodes = (np.arange(512) + 0.5) * np.pi / 512
    waves = np.exp(-1j * (angle * SUB / 2)[:, None] * np.cos(nodes)[None, :])
    coefs = (2.0 / 512) * waves @ np.cos(nodes[:, None] * np.arange(Q)[None, :])
    coefs[:, 0] /= 2
    starts = np.arange(length // SUB) * SUB + (SUB - 1) / 2
    shift = np.exp(-1j * starts[:, None] * angle[None, :])
    return (shift[:, None, :] * coefs.T[None, :, :]).reshape(-1, len(freqs))


def two_parts(values):
    high = values.astype(ml_dtypes.bfloat16)
    low = (values - high.astype(np.float64)).astype(ml_dtypes.bfloat16)
    return high, low


def z_table():
    factors = twiddle_factors(np.arange(HALF) * (np.arange(HALF) <= 64), NZ)
    return np.concatenate(two_parts(np.concatenate([factors.real, factors.imag], axis=1).T))


def y_table():
    factors = twiddle_factors(np.arange(KY) - KY // 2, NY)
    real, imag = factors.real, factors.imag
    both = np.stack(
        [np.concatenate([real, imag], axis=1), np.concatenate([-imag, real], axis=1)]
    )
    return np.stack(two_parts(both))


def split(values):
    high = values.astype(jnp.bfloat16)
    return high, (values - high.astype(jnp.float32)).astype(jnp.bfloat16)


def dot(a, b):
    return jnp.dot(a, b, preferred_element_type=jnp.float32)


def tile_blocks(dest_ref, first_ref, second_ref):
    lane = lax.broadcasted_iota(jnp.int32, (PL, SUB), 1)
    plane = lax.broadcasted_iota(jnp.int32, (PL, SUB), 0)
    dest = [jnp.broadcast_to(dest_ref[r : r + 1, :], (PL, SUB)) for r in range(8)]

    def find(step, carry):
        first, second = carry
        for j in range(8):
            device = step * 8 + j
            tile = device * PL + plane
            most = total = jnp.zeros((PL, SUB), jnp.int32)
            for r in range(8):
                named = jnp.where(dest[r] == tile, lane + (SUB * r + 1), 0)
                most, total = jnp.maximum(most, named), total + named
            most = jnp.max(most, axis=1, keepdims=True)
            total = jnp.sum(total, axis=1, keepdims=True)
            first = jnp.where(lane == device, most, first)
            second = jnp.where(lane == device, jnp.minimum(total - most, PL * SUB), second)
        return first, second

    none = jnp.zeros((PL, SUB), jnp.int32)
    first_ref[...], second_ref[...] = lax.fori_loop(0, DEVICES // 8, find, (none, none))


def chain(ref, first, x):
    twice = x + x
    before, now = first, first * x
    ref[0:8, :] = before
    ref[8:16, :] = now
    for q in range(2, Q):
        before, now = now, twice * now - before
        ref[8 * q : 8 * q + 8, :] = now


def block_products(count_ref, cells_ref, mass_ref, blocks, chains):
    blocks[0] = jnp.zeros((Q, SUB), jnp.float32)
    lane = lax.broadcasted_iota(jnp.int32, (8, SUB), 1)
    number = lax.broadcasted_iota(jnp.int32, (8, SUB), 0)

    def step(group, carry):
        none = jnp.zeros((Q, SUB), jnp.bfloat16)
        first = pl.multiple_of(group * UNROLL, UNROLL)
        masses = mass_ref[pl.ds(first, UNROLL), :].astype(jnp.float32)
        counts = jnp.broadcast_to(count_ref[pl.ds(first // SUB, 1), :], (8, SUB))
        for eight in range(UNROLL // 8):
            z_chain, y_chain = chains[2 * eight], chains[2 * eight + 1]
            base = pl.multiple_of(first + 8 * eight, 8)
            cells = cells_ref[pl.ds(base, 8), :]
            count = jnp.take_along_axis(
                counts, number + lax.rem(base, SUB), axis=1, mode="promise_in_bounds"
            )
            weight = jnp.where(lane < count, masses[8 * eight : 8 * eight + 8], 0.0)
            z_at = ((cells & (SUB - 1)).astype(jnp.float32) - (SUB - 1) / 2) * (2 / SUB)
            y_at = (((cells >> 7) & (SUB - 1)).astype(jnp.float32) - (SUB - 1) / 2) * (2 / SUB)
            chain(z_chain, weight, z_at)
            chain(y_chain, jnp.ones_like(weight), y_at)
            lower_half = (cells >> 14).astype(jnp.float32)
            for pair in range(0, 8, 2):
                left, right = [], []
                for j in (pair, pair + 1):
                    rows = [pl.ds(64 * i + j, 8, stride=8) for i in range(Q // 8)]
                    left.append(split(jnp.concatenate([z_chain[r, :] for r in rows], axis=0)))
                    high, low = split(jnp.concatenate([y_chain[r, :] for r in rows], axis=0))
                    second = lower_half[j : j + 1]
                    first_half = (1.0 - second).astype(jnp.bfloat16)
                    second = second.astype(jnp.bfloat16)
                    right.append(
                        jnp.concatenate(
                            [high * first_half, high * second, low * first_half, low * second],
                            axis=0,
                        )
                    )
                left = jnp.concatenate(
                    [
                        jnp.concatenate([left[0][0], left[0][1], none, none], axis=0),
                        jnp.concatenate([none, none, left[1][0], left[1][1]], axis=0),
                    ],
                    axis=1,
                )
                part = lax.dot_general(
                    left,
                    jnp.concatenate(right, axis=1),
                    (((1,), (1,)), ((), ())),
                    preferred_element_type=jnp.float32,
                )
                for j in range(2):
                    blocks[base + (1 + pair + j)] = (
                        part[64 * j : 64 * j + 32] + part[64 * j + 32 : 64 * j + 64]
                    )
        return carry

    lax.fori_loop(0, cells_ref.shape[0] // UNROLL, step, 0)


def plane_modes(plane, first_ref, second_ref, blocks, tiles, half, z_ref, y_ref):
    upper = lax.broadcasted_iota(jnp.int32, (Q, SUB), 1) >= SUB // 2

    def named(device):
        return blocks[first_ref[plane, device]] + blocks[second_ref[plane, device]]

    def collect(step, carry):
        for j in range(4):
            col = step * 4 + j
            row = pl.multiple_of(col * Q, Q)
            for i in range(4):
                even = named(2 * i * N_PY + col)
                odd = named((2 * i + 1) * N_PY + col)
                tile = jnp.where(upper, odd, even)
                tile = tile + pltpu.roll(jnp.where(upper, even, odd), SUB // 2, 1)
                high, low = split(tile)
                tiles[pl.ds(row, Q), 256 * i : 256 * i + 128] = high
                tiles[pl.ds(row, Q), 256 * i + 128 : 256 * i + 256] = low
        return carry

    lax.fori_loop(0, N_PY // 4, collect, 0)
    for i in range(4):
        product = dot(z_ref[0:ROWS, :], tiles[:, 256 * i : 256 * i + 256])
        product = product[:, :SUB] + product[:, SUB:]
        product += dot(z_ref[ROWS:, :], tiles[:, 256 * i : 256 * i + 128])
        half[:, SUB * i : SUB * i + SUB] = product
    modes = []
    for c in range(2):
        high, low = split(half[HALF * c : HALF * c + HALF, :])
        modes.append(dot(high, y_ref[0, c]) + dot(low, y_ref[0, c]) + dot(high, y_ref[1, c]))
    plus, minus = modes[0] + modes[1], modes[0] - modes[1]
    last = jnp.broadcast_to(minus[64:65], (8, 2 * KY))
    top = lax.broadcasted_iota(jnp.int32, (8, 2 * KY), 0) == 0
    rows = jnp.concatenate([plus[:64], jnp.where(top, last, minus[:8]), minus[8:64]], axis=0)
    return [rows[:, :KY], rows[:, KY:]]


def slot_of(device):
    ahead = device // 64
    return ahead * (device - 64) + (1 - ahead) * (64 + lax.rem(128 - device, 64))


def mesh_kernel(
    dest_hbm, count_hbm, screen_ref, cells_hbm, mass_hbm, z_hbm, y_hbm, wave_hbm, out_ref,
    dest, count, cells, mass, z_ref, y_ref, wave, first, second, first_at, second_at,
    blocks, tiles, half, give, get, send, landed,
    load_sems, table_sems, give_sems, get_sems, send_sem, land_sem, *chains,
):
    px, py = lax.axis_index("px"), lax.axis_index("py")
    me = px * N_PY + py
    core = lax.rem(px, 2)
    sibling = px + 1 - 2 * core
    loads = [
        pltpu.make_async_copy(a, b, load_sems.at[i])
        for i, (a, b) in enumerate(
            [
                (dest_hbm, dest),
                (count_hbm, count),
                (cells_hbm, cells),
                (mass_hbm, mass),
                (z_hbm, z_ref),
                (y_hbm, y_ref),
                (wave_hbm.at[pl.ds(me, 1)], wave),
            ]
        )
    ]
    for load in loads:
        load.start()
    barrier = pltpu.get_barrier_semaphore()

    def greet(k, carry):
        to = lax.rem(me + k, DEVICES)
        pl.semaphore_signal(barrier, inc=1, device_id=(to // N_PY, to % N_PY), device_id_type=MESH)
        return carry

    lax.fori_loop(1, DEVICES, greet, 0)
    loads[0].wait()
    tile_blocks(dest, first, second)
    tables = [
        pltpu.make_async_copy(first, first_at, table_sems.at[0]),
        pltpu.make_async_copy(second, second_at, table_sems.at[1]),
    ]
    for table in tables:
        table.start()
    for load in loads[1:4]:
        load.wait()
    block_products(count, cells, mass, blocks, chains)
    for copy in loads[4:] + tables:
        copy.wait()
    pl.semaphore_wait(barrier, DEVICES - 1)

    def handover(j):
        rows = pl.ds(pl.multiple_of(j * 256, 256), 256)
        return pltpu.make_async_remote_copy(
            src_ref=give.at[rows],
            dst_ref=get.at[rows],
            send_sem=give_sems.at[j],
            recv_sem=get_sems.at[j],
            device_id=(sibling, py),
            device_id_type=MESH,
        )

    def other_plane(j, carry):
        plane = (1 - core) * HELD + j
        modes = plane_modes(plane, first_at, second_at, blocks, tiles, half, z_ref, y_ref)
        for c in range(2):
            give[pl.ds(pl.multiple_of(j * 256 + 128 * c, 128), 128), :] = modes[c]
        handover(j).start()
        return carry

    def own_plane(j, carry):
        plane = core * HELD + j
        modes = plane_modes(plane, first_at, second_at, blocks, tiles, half, z_ref, y_ref)
        handover(j).wait_recv()
        for c in range(2):
            added = modes[c] + get[pl.ds(pl.multiple_of(j * 256 + 128 * c, 128), 128), :]
            send[pl.ds(HELD * c + j, 128, stride=PARTS), :] = added
        return carry

    lax.fori_loop(0, HELD, other_plane, 0)
    lax.fori_loop(0, HELD, own_plane, 0)
    place = pl.multiple_of((core * 64 + (px // 2) * N_PY + py) * PARTS, PARTS)

    def post(k, carry):
        to = lax.rem(me + k, DEVICES)
        pltpu.make_async_remote_copy(
            src_ref=send.at[pl.ds(pl.multiple_of(slot_of(to) * PARTS, PARTS), PARTS)],
            dst_ref=landed.at[pl.ds(place, PARTS)],
            send_sem=send_sem,
            recv_sem=land_sem,
            device_id=(to // N_PY, to % N_PY),
            device_id_type=MESH,
        ).start()
        return carry

    lax.fori_loop(1, DEVICES, post, 0)
    landed[pl.ds(place, PARTS), :] = send[
        pl.ds(pl.multiple_of(slot_of(me) * PARTS, PARTS), PARTS), :
    ]
    bulk = landed.at[pl.ds(0, (DEVICES - 1) * PARTS)]
    pltpu.make_async_copy(bulk, bulk, land_sem).wait()
    for h in range(2):
        total = jnp.sum(landed[512 * h : 512 * h + 512, :].reshape(64, PARTS, KY), axis=0)
        for j in range(HELD):
            scr = screen_ref[HELD * h + j]
            wave_sq = wave[...]
            green = jnp.where(wave_sq == 0.0, 0.0, -scr / (wave_sq + scr))
            green = green * (1.0 / math.sqrt(NY * NZ))
            for c in range(2):
                row = total[HELD * c + j : HELD * c + j + 1, :]
                out_ref[HELD * h + j, c : c + 1, :] = row * green
    pltpu.make_async_copy(bulk, bulk, send_sem).wait()

    def sent(j, carry):
        handover(j).wait_send()
        return carry

    lax.fori_loop(0, HELD, sent, 0)


def wave_table():
    z_wave = (2.0 * np.sin(np.pi * (np.arange(KZ) - KZ // 2) / NZ)) ** 2
    y_wave = (2.0 * np.sin(np.pi * (np.arange(KY) - KY // 2) / NY)) ** 2
    return (z_wave[:, None] + y_wave[None, :]).astype(np.float32)


def shards(cell_ids, masses, block_dest, block_count, screen):
    blocks = cell_ids.shape[0]
    f32, bf16, i32 = jnp.float32, jnp.bfloat16, jnp.int32
    dma = pltpu.SemaphoreType.DMA
    modes = pl.pallas_call(
        mesh_kernel,
        out_shape=jax.ShapeDtypeStruct((PL, 2, KY), f32),
        in_specs=[
            pl.BlockSpec(memory_space=pltpu.SMEM if i == 2 else pl.ANY) for i in range(8)
        ],
        out_specs=pl.BlockSpec(memory_space=pltpu.VMEM),
        scratch_shapes=[
            pltpu.VMEM((8, SUB), i32),
            pltpu.VMEM((8, SUB), i32),
            pltpu.VMEM((blocks, SUB), i32),
            pltpu.VMEM((blocks, SUB), bf16),
            pltpu.VMEM((2 * ROWS, SPAN), bf16),
            pltpu.VMEM((2, 2, SPAN, 2 * KY), bf16),
            pltpu.VMEM((1, KY), f32),
            pltpu.VMEM((8, SUB), i32),
            pltpu.VMEM((8, SUB), i32),
            pltpu.SMEM((8, SUB), i32),
            pltpu.SMEM((8, SUB), i32),
            pltpu.VMEM((blocks + 1, Q, SUB), f32),
            pltpu.VMEM((SPAN, 8 * SUB), bf16),
            pltpu.VMEM((ROWS, SPAN), f32),
            pltpu.VMEM((HELD * 256, KY), f32),
            pltpu.VMEM((HELD * 256, KY), f32),
            pltpu.VMEM((DEVICES * PARTS, KY), f32),
            pltpu.VMEM((DEVICES * PARTS, KY), f32),
            dma((7,)),
            dma((2,)),
            dma((HELD,)),
            dma((HELD,)),
            dma,
            dma,
        ]
        + [pltpu.VMEM((Q * 8, SUB), f32)] * (UNROLL // 4),
        compiler_params=pltpu.CompilerParams(
            collective_id=0, has_side_effects=True, vmem_limit_bytes=48 << 20
        ),
    )(
        block_dest.reshape(8, SUB),
        block_count.reshape(8, SUB),
        screen,
        cell_ids,
        masses,
        jnp.asarray(z_table()),
        jnp.asarray(y_table()),
        jnp.asarray(wave_table()),
    )
    return jnp.swapaxes(modes, 1, 2)


def solution(mesh):
    return jax.shard_map(
        shards,
        mesh=mesh,
        in_specs=(
            P(("px", "py"), None),
            P(("px", "py"), None),
            P(("px", "py"), None),
            P(("px", "py")),
            P(),
        ),
        out_specs=P(None, None, ("px", "py")),
        check_vma=False,
    )
```

```python
import math

import jax
import jax.numpy as jnp
import ml_dtypes
import numpy as np
from jax import lax
from jax.experimental import pallas as pl
from jax.experimental.pallas import tpu as pltpu
from jax.sharding import PartitionSpec as P

NY = 2048
NZ = 2048
PL = 8
KY = 128
KZ = 128
N_PX = 8
N_PY = 16
DEVICES = N_PX * N_PY
SUB = 128
Q = 32
UNROLL = 64
SPAN = N_PY * Q
ROWS = 144
MEET = 80
HELD = PL // 2
PARTS = 2 * HELD

MESH = pl.DeviceIdType.MESH


def twiddle_factors(freqs, length):
    angle = 2.0 * np.pi * freqs / length
    nodes = (np.arange(512) + 0.5) * np.pi / 512
    waves = np.exp(-1j * (angle * SUB / 2)[:, None] * np.cos(nodes)[None, :])
    coefs = (2.0 / 512) * waves @ np.cos(nodes[:, None] * np.arange(Q)[None, :])
    coefs[:, 0] /= 2
    starts = np.arange(length // SUB) * SUB + (SUB - 1) / 2
    shift = np.exp(-1j * starts[:, None] * angle[None, :])
    return (shift[:, None, :] * coefs.T[None, :, :]).reshape(-1, len(freqs))


def two_parts(values):
    high = values.astype(ml_dtypes.bfloat16)
    low = (values - high.astype(np.float64)).astype(ml_dtypes.bfloat16)
    return high, low


def z_table():
    factors = twiddle_factors(np.arange(65), NZ)
    real, imag = factors.real.T, factors.imag.T
    rows = [real[:64], imag[:64], real[64:], imag[64:], np.zeros((ROWS - 130, SPAN))]
    return np.concatenate(two_parts(np.concatenate(rows)))


def y_table():
    factors = twiddle_factors(np.arange(KY) - KY // 2, NY)
    real, imag = factors.real, factors.imag
    both = [np.concatenate([real, imag], axis=1), np.concatenate([-imag, real], axis=1)]
    parts = [two_parts(table) for table in both]
    return np.stack([np.concatenate([high, high, low]) for high, low in parts])


def split(values):
    high = values.astype(jnp.bfloat16)
    return high, (values - high.astype(jnp.float32)).astype(jnp.bfloat16)


def dot(a, b):
    return jnp.dot(a, b, preferred_element_type=jnp.float32)


def tile_blocks(step, dest_ref, first_ref, second_ref):
    lane = lax.broadcasted_iota(jnp.int32, (PL, SUB), 1)
    plane = lax.broadcasted_iota(jnp.int32, (PL, SUB), 0)
    first, second = first_ref[...], second_ref[...]
    for j in range(8):
        device = step * 8 + j
        tile = device * PL + plane
        most = total = jnp.zeros((PL, SUB), jnp.int32)
        for r in range(8):
            dest = jnp.broadcast_to(dest_ref[r : r + 1, :], (PL, SUB))
            named = jnp.where(dest == tile, lane + (SUB * r + 1), 0)
            most, total = jnp.maximum(most, named), total + named
        most = jnp.max(most, axis=1, keepdims=True)
        total = jnp.sum(total, axis=1, keepdims=True)
        first = jnp.where(lane == device, most, first)
        second = jnp.where(lane == device, jnp.minimum(total - most, PL * SUB), second)
    first_ref[...], second_ref[...] = first, second


def chain(ref, first, x):
    twice = x + x
    before, now = first, first * x
    ref[0:8, :] = before
    ref[8:16, :] = now
    for q in range(2, Q):
        before, now = now, twice * now - before
        ref[8 * q : 8 * q + 8, :] = now


def block_products(count_ref, cells_ref, mass_ref, blocks, chains, beside):
    blocks[0] = jnp.zeros((Q, SUB), jnp.float32)
    lane = lax.broadcasted_iota(jnp.int32, (8, SUB), 1)
    number = lax.broadcasted_iota(jnp.int32, (8, SUB), 0)

    def step(group, carry):
        none = jnp.zeros((Q, SUB), jnp.bfloat16)
        beside(group)
        first = pl.multiple_of(group * UNROLL, UNROLL)
        masses = mass_ref[pl.ds(first, UNROLL), :].astype(jnp.float32)
        counts = jnp.broadcast_to(count_ref[pl.ds(first // SUB, 1), :], (8, SUB))
        for eight in range(UNROLL // 8):
            z_chain, y_chain = chains[2 * eight], chains[2 * eight + 1]
            base = pl.multiple_of(first + 8 * eight, 8)
            cells = cells_ref[pl.ds(base, 8), :]
            count = jnp.take_along_axis(
                counts, number + lax.rem(base, SUB), axis=1, mode="promise_in_bounds"
            )
            weight = jnp.where(lane < count, masses[8 * eight : 8 * eight + 8], 0.0)
            z_at = ((cells & (SUB - 1)).astype(jnp.float32) - (SUB - 1) / 2) * (2 / SUB)
            y_at = (((cells >> 7) & (SUB - 1)).astype(jnp.float32) - (SUB - 1) / 2) * (2 / SUB)
            chain(z_chain, weight, z_at)
            chain(y_chain, jnp.ones_like(weight), y_at)
            lower_half = (cells >> 14).astype(jnp.float32)
            for pair in range(0, 8, 2):
                left, right = [], []
                for j in (pair, pair + 1):
                    rows = [pl.ds(64 * i + j, 8, stride=8) for i in range(Q // 8)]
                    left.append(split(jnp.concatenate([z_chain[r, :] for r in rows], axis=0)))
                    high, low = split(jnp.concatenate([y_chain[r, :] for r in rows], axis=0))
                    second = lower_half[j : j + 1]
                    first_half = (1.0 - second).astype(jnp.bfloat16)
                    second = second.astype(jnp.bfloat16)
                    right.append(
                        jnp.concatenate(
                            [high * first_half, high * second, low * first_half, low * second],
                            axis=0,
                        )
                    )
                left = jnp.concatenate(
                    [
                        jnp.concatenate([left[0][0], left[0][1], none, none], axis=0),
                        jnp.concatenate([none, none, left[1][0], left[1][1]], axis=0),
                    ],
                    axis=1,
                )
                part = lax.dot_general(
                    left,
                    jnp.concatenate(right, axis=1),
                    (((1,), (1,)), ((), ())),
                    preferred_element_type=jnp.float32,
                )
                for j in range(2):
                    blocks[base + (1 + pair + j)] = (
                        part[64 * j : 64 * j + 32] + part[64 * j + 32 : 64 * j + 64]
                    )
        return carry

    lax.fori_loop(0, cells_ref.shape[0] // UNROLL, step, 0)


def collect(plane, first_ref, second_ref, blocks, tiles):
    upper = lax.broadcasted_iota(jnp.int32, (Q, SUB), 1) >= SUB // 2

    def named(device):
        return blocks[first_ref[plane, device]] + blocks[second_ref[plane, device]]

    for col in range(N_PY):
        for i in range(4):
            even = named(2 * i * N_PY + col)
            odd = named((2 * i + 1) * N_PY + col)
            tile = jnp.where(upper, odd, even)
            tile = tile + pltpu.roll(jnp.where(upper, even, odd), SUB // 2, 1)
            for part, values in enumerate(split(tile)):
                tiles[part, Q * col : Q * col + Q, SUB * i : SUB * i + SUB] = values


def z_transform(j, tiles, half, z_ref):
    for n in range(2):
        lanes = slice(256 * n, 256 * n + 256)
        product = dot(z_ref[...], tiles[0, :, lanes])
        product = product[:ROWS] + product[ROWS:] + dot(z_ref[:ROWS, :], tiles[1, :, lanes])
        high, low = split(product)
        for c in range(2):
            for place, part in enumerate((high, low, high)):
                at = slice(SPAN * place + 256 * n, SPAN * place + 256 * n + 256)
                half[c, MEET * j : MEET * j + 64, at] = part[64 * c : 64 * c + 64]
                half[c, MEET * j + 64 : MEET * j + MEET, at] = part[128:ROWS]


def y_transform(half, y_ref, stage):
    real, imag = dot(half[0], y_ref[0]), dot(half[1], y_ref[1])
    top = lax.broadcasted_iota(jnp.int32, (8, 2 * KY), 0) == 0
    for j in range(HELD):
        a, b = real[MEET * j : MEET * j + MEET], imag[MEET * j : MEET * j + MEET]
        minus = a[:64] - b[:64]
        last = jnp.broadcast_to(a[64:65] - b[65:66], (8, 2 * KY))
        minus = jnp.concatenate([jnp.where(top, last, minus[:8]), minus[8:]], axis=0)
        for c in range(2):
            lanes = slice(KY * c, KY * c + KY)
            stage[j, c, 0:64, :] = (a[:64] + b[:64])[:, lanes]
            stage[j, c, 64:128, :] = minus[:, lanes]


def slot_of(device):
    ahead = device >> 6
    return ahead * (device - 64) + (1 - ahead) * (64 + ((128 - device) & 63))


def mesh_kernel(
    dest_hbm, count_hbm, screen_ref, cells_hbm, mass_hbm, z_hbm, y_hbm, wave_hbm, out_ref,
    dest, count, cells, mass, z_ref, y_ref, wave, first, second, first_at, second_at,
    blocks, tiles_a, tiles_b, half, stage, get, send, landed,
    load_sems, table_sems, give_sem, get_sem, send_sem, land_sem, *chains,
):
    px, py = lax.axis_index("px"), lax.axis_index("py")
    me = px * N_PY + py
    core = lax.rem(px, 2)
    sibling = px + 1 - 2 * core
    loads = [
        pltpu.make_async_copy(a, b, load_sems.at[i])
        for i, (a, b) in enumerate(
            [
                (dest_hbm, dest),
                (count_hbm, count),
                (cells_hbm, cells),
                (mass_hbm, mass),
                (z_hbm, z_ref),
                (y_hbm, y_ref),
                (wave_hbm.at[pl.ds(me, 1)], wave),
            ]
        )
    ]
    for load in loads:
        load.start()
    barrier = pltpu.get_barrier_semaphore()

    def greet(k):
        to = (me + k) & (DEVICES - 1)
        pl.semaphore_signal(
            barrier, inc=1, device_id=(to >> 4, to & (N_PY - 1)), device_id_type=MESH
        )

    for k in range(1, 16):
        greet(k)
    first[...] = jnp.zeros_like(first)
    second[...] = jnp.zeros_like(second)

    def beside(group):
        for j in range(7):
            greet(16 + group * 7 + j)
        tile_blocks(group, dest, first, second)

    for load in loads[:4]:
        load.wait()
    block_products(count, cells, mass, blocks, chains, beside)
    tables = [
        pltpu.make_async_copy(first, first_at, table_sems.at[0]),
        pltpu.make_async_copy(second, second_at, table_sems.at[1]),
    ]
    for table in tables:
        table.start()
    for copy in loads[4:] + tables:
        copy.wait()
    handover = pltpu.make_async_remote_copy(
        src_ref=stage.at[0],
        dst_ref=get,
        send_sem=give_sem,
        recv_sem=get_sem,
        device_id=(sibling, py),
        device_id_type=MESH,
    )

    def batch(b, carry):
        base = HELD * (b * core + (1 - b) * (1 - core))
        tiles = (tiles_a, tiles_b)
        collect(base, first_at, second_at, blocks, tiles[0])
        for j in range(HELD):
            z_transform(j, tiles[j % 2], half, z_ref)
            if j + 1 < HELD:
                collect(base + (j + 1), first_at, second_at, blocks, tiles[(j + 1) % 2])
        y_transform(half, y_ref, stage.at[b])

        @pl.when(b == 0)
        def _():
            pl.semaphore_wait(barrier, DEVICES - 1)
            handover.start()

        return carry

    lax.fori_loop(0, 2, batch, 0)
    handover.wait_recv()
    for j in range(HELD):
        for c in range(2):
            send[pl.ds(HELD * c + j, 128, stride=PARTS), :] = stage[1, j, c] + get[j, c]
    place = pl.multiple_of((core * 64 + (px // 2) * N_PY + py) * PARTS, PARTS)

    def post(k, carry):
        to = (me + k) & (DEVICES - 1)
        pltpu.make_async_remote_copy(
            src_ref=send.at[pl.ds(pl.multiple_of(slot_of(to) * PARTS, PARTS), PARTS)],
            dst_ref=landed.at[pl.ds(place, PARTS)],
            send_sem=send_sem,
            recv_sem=land_sem,
            device_id=(to >> 4, to & (N_PY - 1)),
            device_id_type=MESH,
        ).start()
        return carry

    lax.fori_loop(1, DEVICES, post, 0)
    landed[pl.ds(place, PARTS), :] = send[
        pl.ds(pl.multiple_of(slot_of(me) * PARTS, PARTS), PARTS), :
    ]
    bulk = landed.at[pl.ds(0, (DEVICES - 1) * PARTS)]
    pltpu.make_async_copy(bulk, bulk, land_sem).wait()
    for h in range(2):
        total = jnp.sum(landed[512 * h : 512 * h + 512, :].reshape(64, PARTS, KY), axis=0)
        for j in range(HELD):
            scr = screen_ref[HELD * h + j]
            wave_sq = wave[...]
            green = jnp.where(wave_sq == 0.0, 0.0, -scr / (wave_sq + scr))
            green = green * (1.0 / math.sqrt(NY * NZ))
            for c in range(2):
                row = total[HELD * c + j : HELD * c + j + 1, :]
                out_ref[HELD * h + j, c : c + 1, :] = row * green
    pltpu.make_async_copy(bulk, bulk, send_sem).wait()
    handover.wait_send()


def wave_table():
    z_wave = (2.0 * np.sin(np.pi * (np.arange(KZ) - KZ // 2) / NZ)) ** 2
    y_wave = (2.0 * np.sin(np.pi * (np.arange(KY) - KY // 2) / NY)) ** 2
    return (z_wave[:, None] + y_wave[None, :]).astype(np.float32)


def shards(cell_ids, masses, block_dest, block_count, screen):
    blocks = cell_ids.shape[0]
    f32, bf16, i32 = jnp.float32, jnp.bfloat16, jnp.int32
    dma = pltpu.SemaphoreType.DMA
    modes = pl.pallas_call(
        mesh_kernel,
        out_shape=jax.ShapeDtypeStruct((PL, 2, KY), f32),
        in_specs=[
            pl.BlockSpec(memory_space=pltpu.SMEM if i == 2 else pl.ANY) for i in range(8)
        ],
        out_specs=pl.BlockSpec(memory_space=pltpu.VMEM),
        scratch_shapes=[
            pltpu.VMEM((8, SUB), i32),
            pltpu.VMEM((8, SUB), i32),
            pltpu.VMEM((blocks, SUB), i32),
            pltpu.VMEM((blocks, SUB), bf16),
            pltpu.VMEM((2 * ROWS, SPAN), bf16),
            pltpu.VMEM((2, 3 * SPAN, 2 * KY), bf16),
            pltpu.VMEM((1, KY), f32),
            pltpu.VMEM((8, SUB), i32),
            pltpu.VMEM((8, SUB), i32),
            pltpu.SMEM((8, SUB), i32),
            pltpu.SMEM((8, SUB), i32),
            pltpu.VMEM((blocks + 1, Q, SUB), f32),
            pltpu.VMEM((2, SPAN, SPAN), bf16),
            pltpu.VMEM((2, SPAN, SPAN), bf16),
            pltpu.VMEM((2, HELD * MEET, 3 * SPAN), bf16),
            pltpu.VMEM((2, HELD, 2, KZ, KY), f32),
            pltpu.VMEM((HELD, 2, KZ, KY), f32),
            pltpu.VMEM((DEVICES * PARTS, KY), f32),
            pltpu.VMEM((DEVICES * PARTS, KY), f32),
            dma((7,)),
            dma((2,)),
            dma,
            dma,
            dma,
            dma,
        ]
        + [pltpu.VMEM((Q * 8, SUB), f32)] * (UNROLL // 4),
        compiler_params=pltpu.CompilerParams(
            collective_id=0, has_side_effects=True, vmem_limit_bytes=60 << 20
        ),
    )(
        block_dest.reshape(8, SUB),
        block_count.reshape(8, SUB),
        screen,
        cell_ids,
        masses,
        jnp.asarray(z_table()),
        jnp.asarray(y_table()),
        jnp.asarray(wave_table()),
    )
    return jnp.swapaxes(modes, 1, 2)


def solution(mesh):
    return jax.shard_map(
        shards,
        mesh=mesh,
        in_specs=(
            P(("px", "py"), None),
            P(("px", "py"), None),
            P(("px", "py"), None),
            P(("px", "py")),
            P(),
        ),
        out_specs=P(None, None, ("px", "py")),
        check_vma=False,
    )
```

```python
import math

import jax
import jax.numpy as jnp
import ml_dtypes
import numpy as np
from jax import lax
from jax.experimental import pallas as pl
from jax.experimental.pallas import tpu as pltpu
from jax.sharding import PartitionSpec as P

NY = 2048
NZ = 2048
PL = 8
KY = 128
KZ = 128
N_PX = 8
N_PY = 16
DEVICES = N_PX * N_PY
SUB = 128
Q = 32
UNROLL = 128
SPAN = N_PY * Q
ROWS = 144
MEET = 80
HELD = PL // 2
PARTS = 2 * HELD

MESH = pl.DeviceIdType.MESH


def twiddle_factors(freqs, length):
    angle = 2.0 * np.pi * freqs / length
    nodes = (np.arange(512) + 0.5) * np.pi / 512
    waves = np.exp(-1j * (angle * SUB / 2)[:, None] * np.cos(nodes)[None, :])
    coefs = (2.0 / 512) * waves @ np.cos(nodes[:, None] * np.arange(Q)[None, :])
    coefs[:, 0] /= 2
    starts = np.arange(length // SUB) * SUB + (SUB - 1) / 2
    shift = np.exp(-1j * starts[:, None] * angle[None, :])
    return (shift[:, None, :] * coefs.T[None, :, :]).reshape(-1, len(freqs))


def two_parts(values):
    high = values.astype(ml_dtypes.bfloat16)
    low = (values - high.astype(np.float64)).astype(ml_dtypes.bfloat16)
    return high, low


def z_table():
    factors = twiddle_factors(np.arange(65), NZ)
    real, imag = factors.real.T, factors.imag.T
    rows = [real[:64], imag[:64], real[64:], imag[64:], np.zeros((ROWS - 130, SPAN))]
    return np.concatenate(two_parts(np.concatenate(rows)))


def y_table():
    factors = twiddle_factors(np.arange(KY) - KY // 2, NY)
    real, imag = factors.real, factors.imag
    both = [np.concatenate([real, imag], axis=1), np.concatenate([-imag, real], axis=1)]
    parts = [two_parts(table) for table in both]
    return np.stack([np.concatenate([high, high, low]) for high, low in parts])


def split(values):
    high = values.astype(jnp.bfloat16)
    return high, (values - high.astype(jnp.float32)).astype(jnp.bfloat16)


def dot(a, b):
    return jnp.dot(a, b, preferred_element_type=jnp.float32)


def tile_blocks(step, dest_ref, first_ref, second_ref):
    lane = lax.broadcasted_iota(jnp.int32, (PL, SUB), 1)
    plane = lax.broadcasted_iota(jnp.int32, (PL, SUB), 0)
    first, second = first_ref[...], second_ref[...]
    for j in range(8):
        device = step * 8 + j
        tile = device * PL + plane
        most = total = jnp.zeros((PL, SUB), jnp.int32)
        for r in range(8):
            dest = jnp.broadcast_to(dest_ref[r : r + 1, :], (PL, SUB))
            named = jnp.where(dest == tile, lane + (SUB * r + 1), 0)
            most, total = jnp.maximum(most, named), total + named
        most = jnp.max(most, axis=1, keepdims=True)
        total = jnp.sum(total, axis=1, keepdims=True)
        first = jnp.where(lane == device, most, first)
        second = jnp.where(lane == device, jnp.minimum(total - most, PL * SUB), second)
    first_ref[...], second_ref[...] = first, second


def chain(ref, first, x):
    twice = x + x
    before, now = first, first * x
    ref[0:8, :] = before
    ref[8:16, :] = now
    for q in range(2, Q):
        before, now = now, twice * now - before
        ref[8 * q : 8 * q + 8, :] = now


def block_products(count_ref, cells_ref, mass_ref, blocks, chains, beside, between):
    blocks[0] = jnp.zeros((Q, SUB), jnp.float32)
    lane = lax.broadcasted_iota(jnp.int32, (8, SUB), 1)
    number = lax.broadcasted_iota(jnp.int32, (8, SUB), 0)

    def both(group, carry):
        beside(group)
        return step(group, carry)

    def step(group, carry):
        none = jnp.zeros((Q, SUB), jnp.bfloat16)
        first = pl.multiple_of(group * UNROLL, UNROLL)
        masses = mass_ref[pl.ds(first, UNROLL), :].astype(jnp.float32)
        counts = jnp.broadcast_to(count_ref[pl.ds(first // SUB, 1), :], (8, SUB))
        for eight in range(UNROLL // 8):
            z_chain, y_chain = chains[2 * eight], chains[2 * eight + 1]
            base = pl.multiple_of(first + 8 * eight, 8)
            cells = cells_ref[pl.ds(base, 8), :]
            count = jnp.take_along_axis(
                counts, number + lax.rem(base, SUB), axis=1, mode="promise_in_bounds"
            )
            weight = jnp.where(lane < count, masses[8 * eight : 8 * eight + 8], 0.0)
            z_at = ((cells & (SUB - 1)).astype(jnp.float32) - (SUB - 1) / 2) * (2 / SUB)
            y_at = (((cells >> 7) & (SUB - 1)).astype(jnp.float32) - (SUB - 1) / 2) * (2 / SUB)
            chain(z_chain, weight, z_at)
            chain(y_chain, jnp.ones_like(weight), y_at)
            lower_half = (cells >> 14).astype(jnp.float32)
            for pair in range(0, 8, 2):
                left, right = [], []
                for j in (pair, pair + 1):
                    rows = [pl.ds(64 * i + j, 8, stride=8) for i in range(Q // 8)]
                    left.append(split(jnp.concatenate([z_chain[r, :] for r in rows], axis=0)))
                    high, low = split(jnp.concatenate([y_chain[r, :] for r in rows], axis=0))
                    second = lower_half[j : j + 1]
                    first_half = (1.0 - second).astype(jnp.bfloat16)
                    second = second.astype(jnp.bfloat16)
                    right.append(
                        jnp.concatenate(
                            [high * first_half, high * second, low * first_half, low * second],
                            axis=0,
                        )
                    )
                left = jnp.concatenate(
                    [
                        jnp.concatenate([left[0][0], left[0][1], none, none], axis=0),
                        jnp.concatenate([none, none, left[1][0], left[1][1]], axis=0),
                    ],
                    axis=1,
                )
                part = lax.dot_general(
                    left,
                    jnp.concatenate(right, axis=1),
                    (((1,), (1,)), ((), ())),
                    preferred_element_type=jnp.float32,
                )
                for j in range(2):
                    blocks[base + (1 + pair + j)] = (
                        part[64 * j : 64 * j + 32] + part[64 * j + 32 : 64 * j + 64]
                    )
        return carry

    steps = cells_ref.shape[0] // UNROLL
    lax.fori_loop(0, steps // 2, both, 0)
    between()
    lax.fori_loop(steps // 2, steps, step, 0)


def collect(plane, first_ref, second_ref, blocks, tiles):
    upper = lax.broadcasted_iota(jnp.int32, (Q, SUB), 1) >= SUB // 2

    def named(device):
        return blocks[first_ref[plane, device]] + blocks[second_ref[plane, device]]

    for col in range(N_PY):
        for i in range(4):
            even = named(2 * i * N_PY + col)
            odd = named((2 * i + 1) * N_PY + col)
            tile = jnp.where(upper, odd, even)
            tile = tile + pltpu.roll(jnp.where(upper, even, odd), SUB // 2, 1)
            for part, values in enumerate(split(tile)):
                tiles[part, Q * col : Q * col + Q, SUB * i : SUB * i + SUB] = values


def z_transform(j, tiles, half, z_ref):
    for n in range(2):
        lanes = slice(256 * n, 256 * n + 256)
        product = dot(z_ref[...], tiles[0, :, lanes])
        product = product[:ROWS] + product[ROWS:] + dot(z_ref[:ROWS, :], tiles[1, :, lanes])
        high, low = split(product)
        for c in range(2):
            for place, part in enumerate((high, low, high)):
                at = slice(SPAN * place + 256 * n, SPAN * place + 256 * n + 256)
                half[c, MEET * j : MEET * j + 64, at] = part[64 * c : 64 * c + 64]
                half[c, MEET * j + 64 : MEET * j + MEET, at] = part[128:ROWS]


def y_transform(half, y_ref, stage):
    real, imag = dot(half[0], y_ref[0]), dot(half[1], y_ref[1])
    top = lax.broadcasted_iota(jnp.int32, (8, 2 * KY), 0) == 0
    for j in range(HELD):
        a, b = real[MEET * j : MEET * j + MEET], imag[MEET * j : MEET * j + MEET]
        minus = a[:64] - b[:64]
        last = jnp.broadcast_to(a[64:65] - b[65:66], (8, 2 * KY))
        minus = jnp.concatenate([jnp.where(top, last, minus[:8]), minus[8:]], axis=0)
        for c in range(2):
            lanes = slice(KY * c, KY * c + KY)
            stage[j, c, 0:64, :] = (a[:64] + b[:64])[:, lanes]
            stage[j, c, 64:128, :] = minus[:, lanes]


def slot_of(device):
    ahead = device >> 6
    return ahead * (device - 64) + (1 - ahead) * (64 + ((128 - device) & 63))


def mesh_kernel(
    dest_hbm, count_hbm, screen_ref, cells_hbm, mass_hbm, z_hbm, y_hbm, wave_hbm, out_ref,
    dest, count, cells, mass, z_ref, y_ref, wave, first, second, first_at, second_at,
    blocks, tiles_a, tiles_b, half, stage, get, send, landed,
    load_sems, table_sems, give_sem, get_sem, send_sem, land_sem, *chains,
):
    px, py = lax.axis_index("px"), lax.axis_index("py")
    me = px * N_PY + py
    core = lax.rem(px, 2)
    sibling = px + 1 - 2 * core
    loads = [
        pltpu.make_async_copy(a, b, load_sems.at[i])
        for i, (a, b) in enumerate(
            [
                (dest_hbm, dest),
                (count_hbm, count),
                (cells_hbm, cells),
                (mass_hbm, mass),
                (z_hbm, z_ref),
                (y_hbm, y_ref),
                (wave_hbm.at[pl.ds(me, 1)], wave),
            ]
        )
    ]
    for load in loads:
        load.start()
    barrier = pltpu.get_barrier_semaphore()

    def greet(k):
        to = (me + k) & (DEVICES - 1)
        pl.semaphore_signal(
            barrier, inc=1, device_id=(to >> 4, to & (N_PY - 1)), device_id_type=MESH
        )

    def greet_some(k, carry):
        greet(k)
        return carry

    lax.fori_loop(1, 64, greet_some, 0)
    first[...] = jnp.zeros_like(first)
    second[...] = jnp.zeros_like(second)

    def beside(group):
        for j in range(16):
            greet(64 + group * 16 + j)
        for j in range(4):
            tile_blocks(group * 4 + j, dest, first, second)

    for load in loads[:4]:
        load.wait()
    tables = [
        pltpu.make_async_copy(first, first_at, table_sems.at[0]),
        pltpu.make_async_copy(second, second_at, table_sems.at[1]),
    ]

    def between():
        for table in tables:
            table.start()

    block_products(count, cells, mass, blocks, chains, beside, between)
    for copy in loads[4:] + tables:
        copy.wait()
    handover = pltpu.make_async_remote_copy(
        src_ref=stage.at[0],
        dst_ref=get,
        send_sem=give_sem,
        recv_sem=get_sem,
        device_id=(sibling, py),
        device_id_type=MESH,
    )

    def batch(b, carry):
        base = HELD * (b * core + (1 - b) * (1 - core))
        tiles = (tiles_a, tiles_b)
        collect(base, first_at, second_at, blocks, tiles[0])
        for j in range(HELD):
            z_transform(j, tiles[j % 2], half, z_ref)
            if j + 1 < HELD:
                collect(base + (j + 1), first_at, second_at, blocks, tiles[(j + 1) % 2])
        y_transform(half, y_ref, stage.at[b])

        @pl.when(b == 0)
        def _():
            pl.semaphore_wait(barrier, DEVICES - 1)
            handover.start()

        return carry

    lax.fori_loop(0, 2, batch, 0)
    handover.wait_recv()
    for j in range(HELD):
        for c in range(2):
            send[pl.ds(HELD * c + j, 128, stride=PARTS), :] = stage[1, j, c] + get[j, c]
    place = pl.multiple_of((core * 64 + (px // 2) * N_PY + py) * PARTS, PARTS)

    def post(k, carry):
        to = (me + k) & (DEVICES - 1)
        pltpu.make_async_remote_copy(
            src_ref=send.at[pl.ds(pl.multiple_of(slot_of(to) * PARTS, PARTS), PARTS)],
            dst_ref=landed.at[pl.ds(place, PARTS)],
            send_sem=send_sem,
            recv_sem=land_sem,
            device_id=(to >> 4, to & (N_PY - 1)),
            device_id_type=MESH,
        ).start()
        return carry

    lax.fori_loop(1, DEVICES, post, 0)
    landed[pl.ds(place, PARTS), :] = send[
        pl.ds(pl.multiple_of(slot_of(me) * PARTS, PARTS), PARTS), :
    ]
    bulk = landed.at[pl.ds(0, (DEVICES - 1) * PARTS)]
    pltpu.make_async_copy(bulk, bulk, land_sem).wait()
    for h in range(2):
        total = jnp.sum(landed[512 * h : 512 * h + 512, :].reshape(64, PARTS, KY), axis=0)
        for j in range(HELD):
            scr = screen_ref[HELD * h + j]
            wave_sq = wave[...]
            green = jnp.where(wave_sq == 0.0, 0.0, -scr / (wave_sq + scr))
            green = green * (1.0 / math.sqrt(NY * NZ))
            for c in range(2):
                row = total[HELD * c + j : HELD * c + j + 1, :]
                out_ref[HELD * h + j, c : c + 1, :] = row * green
    pltpu.make_async_copy(bulk, bulk, send_sem).wait()
    handover.wait_send()


def wave_table():
    z_wave = (2.0 * np.sin(np.pi * (np.arange(KZ) - KZ // 2) / NZ)) ** 2
    y_wave = (2.0 * np.sin(np.pi * (np.arange(KY) - KY // 2) / NY)) ** 2
    return (z_wave[:, None] + y_wave[None, :]).astype(np.float32)


def shards(cell_ids, masses, block_dest, block_count, screen):
    blocks = cell_ids.shape[0]
    f32, bf16, i32 = jnp.float32, jnp.bfloat16, jnp.int32
    dma = pltpu.SemaphoreType.DMA
    modes = pl.pallas_call(
        mesh_kernel,
        out_shape=jax.ShapeDtypeStruct((PL, 2, KY), f32),
        in_specs=[
            pl.BlockSpec(memory_space=pltpu.SMEM if i == 2 else pl.ANY) for i in range(8)
        ],
        out_specs=pl.BlockSpec(memory_space=pltpu.VMEM),
        scratch_shapes=[
            pltpu.VMEM((8, SUB), i32),
            pltpu.VMEM((8, SUB), i32),
            pltpu.VMEM((blocks, SUB), i32),
            pltpu.VMEM((blocks, SUB), bf16),
            pltpu.VMEM((2 * ROWS, SPAN), bf16),
            pltpu.VMEM((2, 3 * SPAN, 2 * KY), bf16),
            pltpu.VMEM((1, KY), f32),
            pltpu.VMEM((8, SUB), i32),
            pltpu.VMEM((8, SUB), i32),
            pltpu.SMEM((8, SUB), i32),
            pltpu.SMEM((8, SUB), i32),
            pltpu.VMEM((blocks + 1, Q, SUB), f32),
            pltpu.VMEM((2, SPAN, SPAN), bf16),
            pltpu.VMEM((2, SPAN, SPAN), bf16),
            pltpu.VMEM((2, HELD * MEET, 3 * SPAN), bf16),
            pltpu.VMEM((2, HELD, 2, KZ, KY), f32),
            pltpu.VMEM((HELD, 2, KZ, KY), f32),
            pltpu.VMEM((DEVICES * PARTS, KY), f32),
            pltpu.VMEM((DEVICES * PARTS, KY), f32),
            dma((7,)),
            dma((2,)),
            dma,
            dma,
            dma,
            dma,
        ]
        + [pltpu.VMEM((Q * 8, SUB), f32)] * (UNROLL // 4),
        compiler_params=pltpu.CompilerParams(
            collective_id=0, has_side_effects=True, vmem_limit_bytes=60 << 20
        ),
    )(
        block_dest.reshape(8, SUB),
        block_count.reshape(8, SUB),
        screen,
        cell_ids,
        masses,
        jnp.asarray(z_table()),
        jnp.asarray(y_table()),
        jnp.asarray(wave_table()),
    )
    return jnp.swapaxes(modes, 1, 2)


def solution(mesh):
    return jax.shard_map(
        shards,
        mesh=mesh,
        in_specs=(
            P(("px", "py"), None),
            P(("px", "py"), None),
            P(("px", "py"), None),
            P(("px", "py")),
            P(),
        ),
        out_specs=P(None, None, ("px", "py")),
        check_vma=False,
    )
```

```python
import math

import jax
import jax.numpy as jnp
import ml_dtypes
import numpy as np
from jax import lax
from jax.experimental import pallas as pl
from jax.experimental.pallas import tpu as pltpu
from jax.sharding import PartitionSpec as P

NY = 2048
NZ = 2048
PL = 8
KY = 128
KZ = 128
N_PX = 8
N_PY = 16
DEVICES = N_PX * N_PY
SUB = 128
Q = 32
UNROLL = 128
SPAN = N_PY * Q
ROWS = 144
MEET = 80
HELD = PL // 2
PARTS = 2 * HELD

MESH = pl.DeviceIdType.MESH


def twiddle_factors(freqs, length):
    angle = 2.0 * np.pi * freqs / length
    nodes = (np.arange(512) + 0.5) * np.pi / 512
    waves = np.exp(-1j * (angle * SUB / 2)[:, None] * np.cos(nodes)[None, :])
    coefs = (2.0 / 512) * waves @ np.cos(nodes[:, None] * np.arange(Q)[None, :])
    coefs[:, 0] /= 2
    starts = np.arange(length // SUB) * SUB + (SUB - 1) / 2
    shift = np.exp(-1j * starts[:, None] * angle[None, :])
    return (shift[:, None, :] * coefs.T[None, :, :]).reshape(-1, len(freqs))


def two_parts(values):
    high = values.astype(ml_dtypes.bfloat16)
    low = (values - high.astype(np.float64)).astype(ml_dtypes.bfloat16)
    return high, low


def z_table():
    factors = twiddle_factors(np.arange(65), NZ)
    real, imag = factors.real.T, factors.imag.T
    rows = [real[:64], imag[:64], real[64:], imag[64:], np.zeros((ROWS - 130, SPAN))]
    return np.concatenate(two_parts(np.concatenate(rows)))


def y_table():
    factors = twiddle_factors(np.arange(KY) - KY // 2, NY)
    real, imag = factors.real, factors.imag
    both = [np.concatenate([real, imag], axis=1), np.concatenate([-imag, real], axis=1)]
    parts = [two_parts(table) for table in both]
    return np.stack([np.concatenate([high, high, low]) for high, low in parts])


def split(values):
    high = values.astype(jnp.bfloat16)
    return high, (values - high.astype(jnp.float32)).astype(jnp.bfloat16)


def dot(a, b):
    return jnp.dot(a, b, preferred_element_type=jnp.float32)


def merge(a, b, shift, better):
    high = (lax.broadcasted_iota(jnp.int32, (PL, SUB), 1) & shift) != 0
    swapped = jnp.where(high, a, b)
    other = pltpu.roll(swapped, SUB - shift, 1)
    if 2 * shift < SUB:
        other = jnp.where(high, pltpu.roll(swapped, shift, 1), other)
    return better(jnp.where(high, b, a), other)


def merge_all(values, shift, better):
    while len(values) > 1:
        half = len(values) // 2
        values = [merge(values[n], values[n + half], shift, better) for n in range(half)]
        shift //= 2
    return values[0]


def tile_blocks(step, dest_ref, most_ref, least_ref):
    lane = lax.broadcasted_iota(jnp.int32, (PL, SUB), 1)
    plane = lax.broadcasted_iota(jnp.int32, (PL, SUB), 0)
    names = [lane + (SUB * r + 1) for r in range(8)]
    dest = [jnp.broadcast_to(dest_ref[r : r + 1, :], (PL, SUB)) - plane for r in range(8)]
    mosts, leasts = [], []
    for j in range(8):
        named = [dest[r] == (step + 16 * j) * PL for r in range(8)]
        most, least = jnp.zeros((PL, SUB), jnp.int32), jnp.full((PL, SUB), 2 * PL * SUB, jnp.int32)
        for r in range(8):
            most = jnp.where(named[r], names[r], most)
            least = jnp.where(named[7 - r], names[7 - r], least)
        mosts.append(most)
        leasts.append(least)
    most_ref[step] = merge_all(mosts, 64, jnp.maximum)
    least_ref[step] = merge_all(leasts, 64, jnp.minimum)


def tile_table(most_ref, least_ref, first_ref, second_ref):
    most = merge_all([most_ref[n] for n in range(16)], 8, jnp.maximum)
    least = merge_all([least_ref[n] for n in range(16)], 8, jnp.minimum)
    first_ref[...] = most
    second_ref[...] = jnp.where(least < most, least, 0)


def chain(ref, first, x):
    twice = x + x
    before, now = first, first * x
    ref[0:8, :] = before
    ref[8:16, :] = now
    for q in range(2, Q):
        before, now = now, twice * now - before
        ref[8 * q : 8 * q + 8, :] = now


def block_products(count_ref, cells_ref, mass_ref, blocks, chains, beside, between):
    blocks[0] = jnp.zeros((Q, SUB), jnp.float32)
    lane = lax.broadcasted_iota(jnp.int32, (8, SUB), 1)
    number = lax.broadcasted_iota(jnp.int32, (8, SUB), 0)

    def both(group, carry):
        beside(group)
        return step(group, carry)

    def step(group, carry):
        none = jnp.zeros((Q, SUB), jnp.bfloat16)
        first = pl.multiple_of(group * UNROLL, UNROLL)
        masses = mass_ref[pl.ds(first, UNROLL), :].astype(jnp.float32)
        counts = jnp.broadcast_to(count_ref[pl.ds(first // SUB, 1), :], (8, SUB))
        for eight in range(UNROLL // 8):
            z_chain, y_chain = chains[2 * eight], chains[2 * eight + 1]
            base = pl.multiple_of(first + 8 * eight, 8)
            cells = cells_ref[pl.ds(base, 8), :]
            count = jnp.take_along_axis(
                counts, number + lax.rem(base, SUB), axis=1, mode="promise_in_bounds"
            )
            weight = jnp.where(lane < count, masses[8 * eight : 8 * eight + 8], 0.0)
            z_at = ((cells & (SUB - 1)).astype(jnp.float32) - (SUB - 1) / 2) * (2 / SUB)
            y_at = (((cells >> 7) & (SUB - 1)).astype(jnp.float32) - (SUB - 1) / 2) * (2 / SUB)
            chain(z_chain, weight, z_at)
            chain(y_chain, jnp.ones_like(weight), y_at)
            lower_half = (cells >> 14).astype(jnp.float32)
            for pair in range(0, 8, 2):
                left, right = [], []
                for j in (pair, pair + 1):
                    rows = [pl.ds(64 * i + j, 8, stride=8) for i in range(Q // 8)]
                    left.append(split(jnp.concatenate([z_chain[r, :] for r in rows], axis=0)))
                    high, low = split(jnp.concatenate([y_chain[r, :] for r in rows], axis=0))
                    second = lower_half[j : j + 1]
                    first_half = (1.0 - second).astype(jnp.bfloat16)
                    second = second.astype(jnp.bfloat16)
                    right.append(
                        jnp.concatenate(
                            [high * first_half, high * second, low * first_half, low * second],
                            axis=0,
                        )
                    )
                left = jnp.concatenate(
                    [
                        jnp.concatenate([left[0][0], left[0][1], none, none], axis=0),
                        jnp.concatenate([none, none, left[1][0], left[1][1]], axis=0),
                    ],
                    axis=1,
                )
                part = lax.dot_general(
                    left,
                    jnp.concatenate(right, axis=1),
                    (((1,), (1,)), ((), ())),
                    preferred_element_type=jnp.float32,
                )
                for j in range(2):
                    blocks[base + (1 + pair + j)] = (
                        part[64 * j : 64 * j + 32] + part[64 * j + 32 : 64 * j + 64]
                    )
        return carry

    steps = cells_ref.shape[0] // UNROLL
    lax.fori_loop(0, steps // 2, both, 0)
    between()
    lax.fori_loop(steps // 2, steps, step, 0)


def collect(plane, first_ref, second_ref, blocks, tiles):
    upper = lax.broadcasted_iota(jnp.int32, (Q, SUB), 1) >= SUB // 2

    def named(device):
        return blocks[first_ref[plane, device]] + blocks[second_ref[plane, device]]

    for col in range(N_PY):
        for i in range(4):
            even = named(2 * i * N_PY + col)
            odd = named((2 * i + 1) * N_PY + col)
            tile = jnp.where(upper, odd, even)
            tile = tile + pltpu.roll(jnp.where(upper, even, odd), SUB // 2, 1)
            tiles[Q * col : Q * col + Q, SUB * i : SUB * i + SUB] = tile


def z_transform(j, tiles, half, z_ref):
    for n in range(2):
        lanes = slice(256 * n, 256 * n + 256)
        product = 0.0
        for k in range(2):
            depth = slice(256 * k, 256 * k + 256)
            high, low = split(tiles[depth, lanes])
            both = dot(z_ref[:, depth], high)
            product += both[:ROWS] + both[ROWS:] + dot(z_ref[:ROWS, depth], low)
        for c in range(2):
            half[c, MEET * j : MEET * j + 64, lanes] = product[64 * c : 64 * c + 64]
            half[c, MEET * j + 64 : MEET * j + MEET, lanes] = product[128:ROWS]


def y_transform(half, y_ref, stage):
    sides = []
    for c in range(2):
        high, low = split(half[c])
        sides.append(dot(jnp.concatenate([high, low, high], axis=1), y_ref[c]))
    real, imag = sides
    top = lax.broadcasted_iota(jnp.int32, (8, 2 * KY), 0) == 0
    for j in range(HELD):
        a, b = real[MEET * j : MEET * j + MEET], imag[MEET * j : MEET * j + MEET]
        minus = a[:64] - b[:64]
        last = jnp.broadcast_to(a[64:65] - b[65:66], (8, 2 * KY))
        minus = jnp.concatenate([jnp.where(top, last, minus[:8]), minus[8:]], axis=0)
        for c in range(2):
            lanes = slice(KY * c, KY * c + KY)
            stage[j, c, 0:64, :] = (a[:64] + b[:64])[:, lanes]
            stage[j, c, 64:128, :] = minus[:, lanes]


def slot_of(device):
    ahead = device >> 6
    return ahead * (device - 64) + (1 - ahead) * (64 + ((128 - device) & 63))


def mesh_kernel(
    dest_hbm, count_hbm, screen_ref, cells_hbm, mass_hbm, z_hbm, y_hbm, wave_hbm, out_ref,
    dest, count, cells, mass, z_ref, y_ref, wave, most, least, first, second, first_at, second_at,
    blocks, tiles_a, tiles_b, half, stage, get, send, landed,
    load_sems, table_sems, give_sem, get_sem, send_sem, land_sem, *chains,
):
    px, py = lax.axis_index("px"), lax.axis_index("py")
    me = px * N_PY + py
    core = lax.rem(px, 2)
    sibling = px + 1 - 2 * core
    loads = [
        pltpu.make_async_copy(a, b, load_sems.at[i])
        for i, (a, b) in enumerate(
            [
                (dest_hbm, dest),
                (count_hbm, count),
                (cells_hbm, cells),
                (mass_hbm, mass),
                (z_hbm, z_ref),
                (y_hbm, y_ref),
                (wave_hbm.at[pl.ds(me, 1)], wave),
            ]
        )
    ]
    for load in loads[:4]:
        load.start()
    barrier = pltpu.get_barrier_semaphore()

    def greet(k):
        to = (me + k) & (DEVICES - 1)
        pl.semaphore_signal(
            barrier, inc=1, device_id=(to >> 4, to & (N_PY - 1)), device_id_type=MESH
        )

    def greet_some(step, carry):
        for j in range(8):
            greet(7 + 8 * step + j)
        return carry

    for k in range(1, 7):
        greet(k)
    lax.fori_loop(0, 15, greet_some, 0)
    greet(DEVICES - 1)

    def beside(group):
        for j in range(4):
            tile_blocks(group * 4 + j, dest, most, least)

    for load in loads[:4]:
        load.wait()
    tables = [
        pltpu.make_async_copy(first, first_at, table_sems.at[0]),
        pltpu.make_async_copy(second, second_at, table_sems.at[1]),
    ]

    def between():
        tile_table(most, least, first, second)
        for copy in tables + loads[4:]:
            copy.start()

    block_products(count, cells, mass, blocks, chains, beside, between)
    for copy in loads[4:] + tables:
        copy.wait()
    handover = pltpu.make_async_remote_copy(
        src_ref=stage.at[0],
        dst_ref=get,
        send_sem=give_sem,
        recv_sem=get_sem,
        device_id=(sibling, py),
        device_id_type=MESH,
    )

    def batch(b, carry):
        base = HELD * (b * core + (1 - b) * (1 - core))
        tiles = (tiles_a, tiles_b)
        collect(base, first_at, second_at, blocks, tiles[0])
        for j in range(HELD):
            z_transform(j, tiles[j % 2], half, z_ref)
            if j + 1 < HELD:
                collect(base + (j + 1), first_at, second_at, blocks, tiles[(j + 1) % 2])
        y_transform(half, y_ref, stage.at[b])

        @pl.when(b == 0)
        def _():
            pl.semaphore_wait(barrier, DEVICES - 1)
            handover.start()

        return carry

    lax.fori_loop(0, 2, batch, 0)
    handover.wait_recv()
    for j in range(HELD):
        for c in range(2):
            send[pl.ds(HELD * c + j, 128, stride=PARTS), :] = stage[1, j, c] + get[j, c]
    place = pl.multiple_of((core * 64 + (px // 2) * N_PY + py) * PARTS, PARTS)

    def post(k, carry):
        to = (me + k) & (DEVICES - 1)
        pltpu.make_async_remote_copy(
            src_ref=send.at[pl.ds(pl.multiple_of(slot_of(to) * PARTS, PARTS), PARTS)],
            dst_ref=landed.at[pl.ds(place, PARTS)],
            send_sem=send_sem,
            recv_sem=land_sem,
            device_id=(to >> 4, to & (N_PY - 1)),
            device_id_type=MESH,
        ).start()
        return carry

    lax.fori_loop(1, DEVICES, post, 0)
    landed[pl.ds(place, PARTS), :] = send[
        pl.ds(pl.multiple_of(slot_of(me) * PARTS, PARTS), PARTS), :
    ]
    bulk = landed.at[pl.ds(0, (DEVICES - 1) * PARTS)]
    pltpu.make_async_copy(bulk, bulk, land_sem).wait()
    for h in range(2):
        total = jnp.sum(landed[512 * h : 512 * h + 512, :].reshape(64, PARTS, KY), axis=0)
        for j in range(HELD):
            scr = screen_ref[HELD * h + j]
            wave_sq = wave[...]
            green = jnp.where(wave_sq == 0.0, 0.0, -scr / (wave_sq + scr))
            green = green * (1.0 / math.sqrt(NY * NZ))
            for c in range(2):
                row = total[HELD * c + j : HELD * c + j + 1, :]
                out_ref[HELD * h + j, c : c + 1, :] = row * green
    pltpu.make_async_copy(bulk, bulk, send_sem).wait()
    handover.wait_send()


def wave_table():
    z_wave = (2.0 * np.sin(np.pi * (np.arange(KZ) - KZ // 2) / NZ)) ** 2
    y_wave = (2.0 * np.sin(np.pi * (np.arange(KY) - KY // 2) / NY)) ** 2
    return (z_wave[:, None] + y_wave[None, :]).astype(np.float32)


def shards(cell_ids, masses, block_dest, block_count, screen):
    blocks = cell_ids.shape[0]
    f32, bf16, i32 = jnp.float32, jnp.bfloat16, jnp.int32
    dma = pltpu.SemaphoreType.DMA
    modes = pl.pallas_call(
        mesh_kernel,
        out_shape=jax.ShapeDtypeStruct((PL, 2, KY), f32),
        in_specs=[
            pl.BlockSpec(memory_space=pltpu.SMEM if i == 2 else pl.ANY) for i in range(8)
        ],
        out_specs=pl.BlockSpec(memory_space=pltpu.VMEM),
        scratch_shapes=[
            pltpu.VMEM((8, SUB), i32),
            pltpu.VMEM((8, SUB), i32),
            pltpu.VMEM((blocks, SUB), i32),
            pltpu.VMEM((blocks, SUB), bf16),
            pltpu.VMEM((2 * ROWS, SPAN), bf16),
            pltpu.VMEM((2, 3 * SPAN, 2 * KY), bf16),
            pltpu.VMEM((1, KY), f32),
            pltpu.VMEM((16, PL, SUB), i32),
            pltpu.VMEM((16, PL, SUB), i32),
            pltpu.VMEM((8, SUB), i32),
            pltpu.VMEM((8, SUB), i32),
            pltpu.SMEM((8, SUB), i32),
            pltpu.SMEM((8, SUB), i32),
            pltpu.VMEM((blocks + 1, Q, SUB), f32),
            pltpu.VMEM((SPAN, SPAN), f32),
            pltpu.VMEM((SPAN, SPAN), f32),
            pltpu.VMEM((2, HELD * MEET, SPAN), f32),
            pltpu.VMEM((2, HELD, 2, KZ, KY), f32),
            pltpu.VMEM((HELD, 2, KZ, KY), f32),
            pltpu.VMEM((DEVICES * PARTS, KY), f32),
            pltpu.VMEM((DEVICES * PARTS, KY), f32),
            dma((7,)),
            dma((2,)),
            dma,
            dma,
            dma,
            dma,
        ]
        + [pltpu.VMEM((Q * 8, SUB), f32)] * (UNROLL // 4),
        compiler_params=pltpu.CompilerParams(
            collective_id=0, has_side_effects=True, vmem_limit_bytes=60 << 20
        ),
    )(
        block_dest.reshape(8, SUB),
        block_count.reshape(8, SUB),
        screen,
        cell_ids,
        masses,
        jnp.asarray(z_table()),
        jnp.asarray(y_table()),
        jnp.asarray(wave_table()),
    )
    return jnp.swapaxes(modes, 1, 2)


def solution(mesh):
    return jax.shard_map(
        shards,
        mesh=mesh,
        in_specs=(
            P(("px", "py"), None),
            P(("px", "py"), None),
            P(("px", "py"), None),
            P(("px", "py")),
            P(),
        ),
        out_specs=P(None, None, ("px", "py")),
        check_vma=False,
    )
```

```python
import math

import jax
import jax.numpy as jnp
import ml_dtypes
import numpy as np
from jax import lax
from jax.experimental import pallas as pl
from jax.experimental.pallas import tpu as pltpu
from jax.sharding import PartitionSpec as P

NY = 2048
NZ = 2048
PL = 8
KY = 128
KZ = 128
N_PX = 8
N_PY = 16
DEVICES = N_PX * N_PY
SUB = 128
Q = 32
UNROLL = 256
SPAN = N_PY * Q
ROWS = 144
MEET = 80
HELD = PL // 2
PARTS = 2 * HELD

MESH = pl.DeviceIdType.MESH


def twiddle_factors(freqs, length):
    angle = 2.0 * np.pi * freqs / length
    nodes = (np.arange(512) + 0.5) * np.pi / 512
    waves = np.exp(-1j * (angle * SUB / 2)[:, None] * np.cos(nodes)[None, :])
    coefs = (2.0 / 512) * waves @ np.cos(nodes[:, None] * np.arange(Q)[None, :])
    coefs[:, 0] /= 2
    starts = np.arange(length // SUB) * SUB + (SUB - 1) / 2
    shift = np.exp(-1j * starts[:, None] * angle[None, :])
    return (shift[:, None, :] * coefs.T[None, :, :]).reshape(-1, len(freqs))


def two_parts(values):
    high = values.astype(ml_dtypes.bfloat16)
    low = (values - high.astype(np.float64)).astype(ml_dtypes.bfloat16)
    return high, low


def z_table():
    factors = twiddle_factors(np.arange(65), NZ)
    real, imag = factors.real.T, factors.imag.T
    rows = [real[:64], imag[:64], real[64:], imag[64:], np.zeros((ROWS - 130, SPAN))]
    return np.concatenate(two_parts(np.concatenate(rows)))


def y_table():
    factors = twiddle_factors(np.arange(KY) - KY // 2, NY)
    real, imag = factors.real, factors.imag
    both = [np.concatenate([real, imag], axis=1), np.concatenate([-imag, real], axis=1)]
    parts = [two_parts(table) for table in both]
    return np.stack([np.concatenate([high, high, low]) for high, low in parts])


def split(values):
    high = values.astype(jnp.bfloat16)
    return high, (values - high.astype(jnp.float32)).astype(jnp.bfloat16)


def dot(a, b):
    return jnp.dot(a, b, preferred_element_type=jnp.float32)


def merge(a, b, shift, better):
    high = (lax.broadcasted_iota(jnp.int32, (PL, SUB), 1) & shift) != 0
    swapped = jnp.where(high, a, b)
    other = pltpu.roll(swapped, SUB - shift, 1)
    if 2 * shift < SUB:
        other = jnp.where(high, pltpu.roll(swapped, shift, 1), other)
    return better(jnp.where(high, b, a), other)


def merge_all(values, shift, better):
    while len(values) > 1:
        half = len(values) // 2
        values = [merge(values[n], values[n + half], shift, better) for n in range(half)]
        shift //= 2
    return values[0]


def tile_blocks(step, dest_ref, most_ref, least_ref):
    lane = lax.broadcasted_iota(jnp.int32, (PL, SUB), 1)
    plane = lax.broadcasted_iota(jnp.int32, (PL, SUB), 0)
    names = [lane + (SUB * r + 1) for r in range(8)]
    dest = [jnp.broadcast_to(dest_ref[r : r + 1, :], (PL, SUB)) - plane for r in range(8)]
    mosts, leasts = [], []
    for j in range(8):
        named = [dest[r] == (step + 16 * j) * PL for r in range(8)]
        most, least = jnp.zeros((PL, SUB), jnp.int32), jnp.full((PL, SUB), 2 * PL * SUB, jnp.int32)
        for r in range(8):
            most = jnp.where(named[r], names[r], most)
            least = jnp.where(named[7 - r], names[7 - r], least)
        mosts.append(most)
        leasts.append(least)
    most_ref[step] = merge_all(mosts, 64, jnp.maximum)
    least_ref[step] = merge_all(leasts, 64, jnp.minimum)


def tile_table(most_ref, least_ref, first_ref, second_ref):
    most = merge_all([most_ref[n] for n in range(16)], 8, jnp.maximum)
    least = merge_all([least_ref[n] for n in range(16)], 8, jnp.minimum)
    first_ref[...] = most
    second_ref[...] = jnp.where(least < most, least, 0)


def chain(ref, first, x):
    twice = x + x
    before, now = first, first * x
    ref[0:8, :] = before
    ref[8:16, :] = now
    for q in range(2, Q):
        before, now = now, twice * now - before
        ref[8 * q : 8 * q + 8, :] = now


def block_products(count_ref, cells_ref, mass_ref, blocks, chains, beside, between):
    blocks[0] = jnp.zeros((Q, SUB), jnp.float32)
    lane = lax.broadcasted_iota(jnp.int32, (8, SUB), 1)
    number = lax.broadcasted_iota(jnp.int32, (8, SUB), 0)

    def both(group, carry):
        beside(group)
        return step(group, carry)

    def step(group, carry):
        none = jnp.zeros((Q, SUB), jnp.bfloat16)
        first = pl.multiple_of(group * UNROLL, UNROLL)
        masses = mass_ref[pl.ds(first, UNROLL), :].astype(jnp.float32)
        counts = [
            jnp.broadcast_to(count_ref[pl.ds(first // SUB + h, 1), :], (8, SUB))
            for h in range(UNROLL // SUB)
        ]
        for eight in range(UNROLL // 8):
            z_chain, y_chain = chains[2 * eight], chains[2 * eight + 1]
            base = pl.multiple_of(first + 8 * eight, 8)
            cells = cells_ref[pl.ds(base, 8), :]
            count = jnp.take_along_axis(
                counts[8 * eight // SUB],
                number + 8 * eight % SUB,
                axis=1,
                mode="promise_in_bounds",
            )
            weight = jnp.where(lane < count, masses[8 * eight : 8 * eight + 8], 0.0)
            z_at = ((cells & (SUB - 1)).astype(jnp.float32) - (SUB - 1) / 2) * (2 / SUB)
            y_at = (((cells >> 7) & (SUB - 1)).astype(jnp.float32) - (SUB - 1) / 2) * (2 / SUB)
            chain(z_chain, weight, z_at)
            chain(y_chain, jnp.ones_like(weight), y_at)
            lower_half = (cells >> 14).astype(jnp.float32)
            for pair in range(0, 8, 2):
                left, right = [], []
                for j in (pair, pair + 1):
                    rows = [pl.ds(64 * i + j, 8, stride=8) for i in range(Q // 8)]
                    left.append(split(jnp.concatenate([z_chain[r, :] for r in rows], axis=0)))
                    high, low = split(jnp.concatenate([y_chain[r, :] for r in rows], axis=0))
                    second = lower_half[j : j + 1]
                    first_half = (1.0 - second).astype(jnp.bfloat16)
                    second = second.astype(jnp.bfloat16)
                    right.append(
                        jnp.concatenate(
                            [high * first_half, high * second, low * first_half, low * second],
                            axis=0,
                        )
                    )
                left = jnp.concatenate(
                    [
                        jnp.concatenate([left[0][0], left[0][1], none, none], axis=0),
                        jnp.concatenate([none, none, left[1][0], left[1][1]], axis=0),
                    ],
                    axis=1,
                )
                part = lax.dot_general(
                    left,
                    jnp.concatenate(right, axis=1),
                    (((1,), (1,)), ((), ())),
                    preferred_element_type=jnp.float32,
                )
                for j in range(2):
                    blocks[base + (1 + pair + j)] = (
                        part[64 * j : 64 * j + 32] + part[64 * j + 32 : 64 * j + 64]
                    )
        return carry

    steps = cells_ref.shape[0] // UNROLL
    lax.fori_loop(0, steps // 2, both, 0)
    between()
    lax.fori_loop(steps // 2, steps, step, 0)


def collect(plane, first_ref, second_ref, blocks, tiles):
    upper = lax.broadcasted_iota(jnp.int32, (Q, SUB), 1) >= SUB // 2

    def named(device):
        return blocks[first_ref[plane, device]] + blocks[second_ref[plane, device]]

    for col in range(N_PY):
        for i in range(4):
            even = named(2 * i * N_PY + col)
            odd = named((2 * i + 1) * N_PY + col)
            tile = jnp.where(upper, odd, even)
            tile = tile + pltpu.roll(jnp.where(upper, even, odd), SUB // 2, 1)
            tiles[Q * col : Q * col + Q, SUB * i : SUB * i + SUB] = tile


def z_transform(j, tiles, half, z_ref):
    for n in range(2):
        lanes = slice(256 * n, 256 * n + 256)
        product = 0.0
        for k in range(2):
            depth = slice(256 * k, 256 * k + 256)
            high, low = split(tiles[depth, lanes])
            both = dot(z_ref[:, depth], high)
            product += both[:ROWS] + both[ROWS:] + dot(z_ref[:ROWS, depth], low)
        for c in range(2):
            half[c, MEET * j : MEET * j + 64, lanes] = product[64 * c : 64 * c + 64]
            half[c, MEET * j + 64 : MEET * j + MEET, lanes] = product[128:ROWS]


def y_transform(half, y_ref, stage):
    sides = []
    for c in range(2):
        high, low = split(half[c])
        sides.append(dot(jnp.concatenate([high, low, high], axis=1), y_ref[c]))
    real, imag = sides
    top = lax.broadcasted_iota(jnp.int32, (8, 2 * KY), 0) == 0
    for j in range(HELD):
        a, b = real[MEET * j : MEET * j + MEET], imag[MEET * j : MEET * j + MEET]
        minus = a[:64] - b[:64]
        last = jnp.broadcast_to(a[64:65] - b[65:66], (8, 2 * KY))
        minus = jnp.concatenate([jnp.where(top, last, minus[:8]), minus[8:]], axis=0)
        for c in range(2):
            lanes = slice(KY * c, KY * c + KY)
            stage[j, c, 0:64, :] = (a[:64] + b[:64])[:, lanes]
            stage[j, c, 64:128, :] = minus[:, lanes]


def slot_of(device):
    ahead = device >> 6
    return ahead * (device - 64) + (1 - ahead) * (64 + ((128 - device) & 63))


def mesh_kernel(
    dest_hbm, count_hbm, screen_ref, cells_hbm, mass_hbm, z_hbm, y_hbm, wave_hbm, out_ref,
    dest, count, cells, mass, z_ref, y_ref, wave, most, least, first, second, first_at, second_at,
    blocks, tiles_a, tiles_b, half, stage, get, send, landed,
    load_sems, table_sems, give_sem, get_sem, send_sem, land_sem, *chains,
):
    px, py = lax.axis_index("px"), lax.axis_index("py")
    me = px * N_PY + py
    core = lax.rem(px, 2)
    sibling = px + 1 - 2 * core
    loads = [
        pltpu.make_async_copy(a, b, load_sems.at[i])
        for i, (a, b) in enumerate(
            [
                (dest_hbm, dest),
                (count_hbm, count),
                (cells_hbm, cells),
                (mass_hbm, mass),
                (z_hbm, z_ref),
                (y_hbm, y_ref),
                (wave_hbm.at[pl.ds(me, 1)], wave),
            ]
        )
    ]
    for load in loads[:4]:
        load.start()
    barrier = pltpu.get_barrier_semaphore()

    def greet(k):
        to = (me + k) & (DEVICES - 1)
        pl.semaphore_signal(
            barrier, inc=1, device_id=(to >> 4, to & (N_PY - 1)), device_id_type=MESH
        )

    def greet_some(step, carry):
        for j in range(8):
            greet(7 + 8 * step + j)
        return carry

    for k in range(1, 7):
        greet(k)
    lax.fori_loop(0, 15, greet_some, 0)
    greet(DEVICES - 1)

    def beside(group):
        for j in range(8):
            tile_blocks(group * 8 + j, dest, most, least)

    for load in loads[:4]:
        load.wait()
    tables = [
        pltpu.make_async_copy(first, first_at, table_sems.at[0]),
        pltpu.make_async_copy(second, second_at, table_sems.at[1]),
    ]

    def between():
        tile_table(most, least, first, second)
        for copy in tables + loads[4:]:
            copy.start()

    block_products(count, cells, mass, blocks, chains, beside, between)
    for copy in loads[4:] + tables:
        copy.wait()
    handover = pltpu.make_async_remote_copy(
        src_ref=stage.at[0],
        dst_ref=get,
        send_sem=give_sem,
        recv_sem=get_sem,
        device_id=(sibling, py),
        device_id_type=MESH,
    )

    def batch(b, carry):
        base = HELD * (b * core + (1 - b) * (1 - core))
        tiles = (tiles_a, tiles_b)
        collect(base, first_at, second_at, blocks, tiles[0])
        for j in range(HELD):
            z_transform(j, tiles[j % 2], half, z_ref)
            if j + 1 < HELD:
                collect(base + (j + 1), first_at, second_at, blocks, tiles[(j + 1) % 2])
        y_transform(half, y_ref, stage.at[b])

        @pl.when(b == 0)
        def _():
            pl.semaphore_wait(barrier, DEVICES - 1)
            handover.start()

        return carry

    lax.fori_loop(0, 2, batch, 0)
    handover.wait_recv()
    for j in range(HELD):
        for c in range(2):
            send[pl.ds(HELD * c + j, 128, stride=PARTS), :] = stage[1, j, c] + get[j, c]
    place = pl.multiple_of((core * 64 + (px // 2) * N_PY + py) * PARTS, PARTS)

    def post(k, carry):
        to = (me + k) & (DEVICES - 1)
        pltpu.make_async_remote_copy(
            src_ref=send.at[pl.ds(pl.multiple_of(slot_of(to) * PARTS, PARTS), PARTS)],
            dst_ref=landed.at[pl.ds(place, PARTS)],
            send_sem=send_sem,
            recv_sem=land_sem,
            device_id=(to >> 4, to & (N_PY - 1)),
            device_id_type=MESH,
        ).start()
        return carry

    lax.fori_loop(1, DEVICES, post, 0)
    landed[pl.ds(place, PARTS), :] = send[
        pl.ds(pl.multiple_of(slot_of(me) * PARTS, PARTS), PARTS), :
    ]
    bulk = landed.at[pl.ds(0, (DEVICES - 1) * PARTS)]
    pltpu.make_async_copy(bulk, bulk, land_sem).wait()
    for h in range(2):
        total = jnp.sum(landed[512 * h : 512 * h + 512, :].reshape(64, PARTS, KY), axis=0)
        for j in range(HELD):
            scr = screen_ref[HELD * h + j]
            wave_sq = wave[...]
            green = jnp.where(wave_sq == 0.0, 0.0, -scr / (wave_sq + scr))
            green = green * (1.0 / math.sqrt(NY * NZ))
            for c in range(2):
                row = total[HELD * c + j : HELD * c + j + 1, :]
                out_ref[HELD * h + j, c : c + 1, :] = row * green
    pltpu.make_async_copy(bulk, bulk, send_sem).wait()
    handover.wait_send()


def wave_table():
    z_wave = (2.0 * np.sin(np.pi * (np.arange(KZ) - KZ // 2) / NZ)) ** 2
    y_wave = (2.0 * np.sin(np.pi * (np.arange(KY) - KY // 2) / NY)) ** 2
    return (z_wave[:, None] + y_wave[None, :]).astype(np.float32)


def shards(cell_ids, masses, block_dest, block_count, screen):
    blocks = cell_ids.shape[0]
    f32, bf16, i32 = jnp.float32, jnp.bfloat16, jnp.int32
    dma = pltpu.SemaphoreType.DMA
    modes = pl.pallas_call(
        mesh_kernel,
        out_shape=jax.ShapeDtypeStruct((PL, 2, KY), f32),
        in_specs=[
            pl.BlockSpec(memory_space=pltpu.SMEM if i == 2 else pl.ANY) for i in range(8)
        ],
        out_specs=pl.BlockSpec(memory_space=pltpu.VMEM),
        scratch_shapes=[
            pltpu.VMEM((8, SUB), i32),
            pltpu.VMEM((8, SUB), i32),
            pltpu.VMEM((blocks, SUB), i32),
            pltpu.VMEM((blocks, SUB), bf16),
            pltpu.VMEM((2 * ROWS, SPAN), bf16),
            pltpu.VMEM((2, 3 * SPAN, 2 * KY), bf16),
            pltpu.VMEM((1, KY), f32),
            pltpu.VMEM((16, PL, SUB), i32),
            pltpu.VMEM((16, PL, SUB), i32),
            pltpu.VMEM((8, SUB), i32),
            pltpu.VMEM((8, SUB), i32),
            pltpu.SMEM((8, SUB), i32),
            pltpu.SMEM((8, SUB), i32),
            pltpu.VMEM((blocks + 1, Q, SUB), f32),
            pltpu.VMEM((SPAN, SPAN), f32),
            pltpu.VMEM((SPAN, SPAN), f32),
            pltpu.VMEM((2, HELD * MEET, SPAN), f32),
            pltpu.VMEM((2, HELD, 2, KZ, KY), f32),
            pltpu.VMEM((HELD, 2, KZ, KY), f32),
            pltpu.VMEM((DEVICES * PARTS, KY), f32),
            pltpu.VMEM((DEVICES * PARTS, KY), f32),
            dma((7,)),
            dma((2,)),
            dma,
            dma,
            dma,
            dma,
        ]
        + [pltpu.VMEM((Q * 8, SUB), f32)] * (UNROLL // 4),
        compiler_params=pltpu.CompilerParams(
            collective_id=0, has_side_effects=True, vmem_limit_bytes=60 << 20
        ),
    )(
        block_dest.reshape(8, SUB),
        block_count.reshape(8, SUB),
        screen,
        cell_ids,
        masses,
        jnp.asarray(z_table()),
        jnp.asarray(y_table()),
        jnp.asarray(wave_table()),
    )
    return jnp.swapaxes(modes, 1, 2)


def solution(mesh):
    return jax.shard_map(
        shards,
        mesh=mesh,
        in_specs=(
            P(("px", "py"), None),
            P(("px", "py"), None),
            P(("px", "py"), None),
            P(("px", "py")),
            P(),
        ),
        out_specs=P(None, None, ("px", "py")),
        check_vma=False,
    )
```

```python
import math

import jax
import jax.numpy as jnp
import ml_dtypes
import numpy as np
from jax import lax
from jax.experimental import pallas as pl
from jax.experimental.pallas import tpu as pltpu
from jax.sharding import PartitionSpec as P

NY = 2048
NZ = 2048
PL = 8
KY = 128
KZ = 128
N_PX = 8
N_PY = 16
DEVICES = N_PX * N_PY
SUB = 128
Q = 32
UNROLL = 256
SPAN = N_PY * Q
ROWS = 144
MEET = 80
HELD = PL // 2
PARTS = 2 * HELD

MESH = pl.DeviceIdType.MESH


def twiddle_factors(freqs, length):
    angle = 2.0 * np.pi * freqs / length
    nodes = (np.arange(512) + 0.5) * np.pi / 512
    waves = np.exp(-1j * (angle * SUB / 2)[:, None] * np.cos(nodes)[None, :])
    coefs = (2.0 / 512) * waves @ np.cos(nodes[:, None] * np.arange(Q)[None, :])
    coefs[:, 0] /= 2
    starts = np.arange(length // SUB) * SUB + (SUB - 1) / 2
    shift = np.exp(-1j * starts[:, None] * angle[None, :])
    return (shift[:, None, :] * coefs.T[None, :, :]).reshape(-1, len(freqs))


def two_parts(values):
    high = values.astype(ml_dtypes.bfloat16)
    low = (values - high.astype(np.float64)).astype(ml_dtypes.bfloat16)
    return high, low


def z_table():
    factors = twiddle_factors(np.arange(65), NZ)
    real, imag = factors.real.T, factors.imag.T
    rows = [real[:64], imag[:64], real[64:], imag[64:], np.zeros((ROWS - 130, SPAN))]
    return np.concatenate(two_parts(np.concatenate(rows)))


def y_table():
    factors = twiddle_factors(np.arange(KY) - KY // 2, NY)
    real, imag = factors.real, factors.imag
    both = [np.concatenate([real, imag], axis=1), np.concatenate([-imag, real], axis=1)]
    parts = [two_parts(table) for table in both]
    return np.stack([np.concatenate([high, high, low]) for high, low in parts])


def split(values):
    high = values.astype(jnp.bfloat16)
    return high, (values - high.astype(jnp.float32)).astype(jnp.bfloat16)


def dot(a, b):
    return jnp.dot(a, b, preferred_element_type=jnp.float32)


def merge(a, b, shift, better):
    high = (lax.broadcasted_iota(jnp.int32, (PL, SUB), 1) & shift) != 0
    swapped = jnp.where(high, a, b)
    other = pltpu.roll(swapped, SUB - shift, 1)
    if 2 * shift < SUB:
        other = jnp.where(high, pltpu.roll(swapped, shift, 1), other)
    return better(jnp.where(high, b, a), other)


def merge_all(values, shift, better):
    while len(values) > 1:
        half = len(values) // 2
        values = [merge(values[n], values[n + half], shift, better) for n in range(half)]
        shift //= 2
    return values[0]


def tile_blocks(step, dest_ref, most_ref, least_ref):
    lane = lax.broadcasted_iota(jnp.int32, (PL, SUB), 1)
    plane = lax.broadcasted_iota(jnp.int32, (PL, SUB), 0)
    names = [lane + (SUB * r + 1) for r in range(8)]
    dest = [jnp.broadcast_to(dest_ref[r : r + 1, :], (PL, SUB)) - plane for r in range(8)]
    mosts, leasts = [], []
    for j in range(8):
        named = [dest[r] == (step + 16 * j) * PL for r in range(8)]
        most, least = jnp.zeros((PL, SUB), jnp.int32), jnp.full((PL, SUB), 2 * PL * SUB, jnp.int32)
        for r in range(8):
            most = jnp.where(named[r], names[r], most)
            least = jnp.where(named[7 - r], names[7 - r], least)
        mosts.append(most)
        leasts.append(least)
    most_ref[step] = merge_all(mosts, 64, jnp.maximum)
    least_ref[step] = merge_all(leasts, 64, jnp.minimum)


def tile_table(most_ref, least_ref, first_ref, second_ref):
    most = merge_all([most_ref[n] for n in range(16)], 8, jnp.maximum)
    least = merge_all([least_ref[n] for n in range(16)], 8, jnp.minimum)
    first_ref[...] = most
    second_ref[...] = jnp.where(least < most, least, 0)


def chain(ref, first, x):
    twice = x + x
    before, now = first, first * x
    ref[0:8, :] = before
    ref[8:16, :] = now
    for q in range(2, Q):
        before, now = now, twice * now - before
        ref[8 * q : 8 * q + 8, :] = now


def block_products(count_ref, cells_ref, mass_ref, blocks, chains, beside, between):
    blocks[0] = jnp.zeros((Q, SUB), jnp.float32)
    lane = lax.broadcasted_iota(jnp.int32, (8, SUB), 1)
    number = lax.broadcasted_iota(jnp.int32, (8, SUB), 0)

    def both(group, carry):
        beside(group)
        return step(group, carry)

    def step(group, carry):
        none = jnp.zeros((Q, SUB), jnp.bfloat16)
        first = pl.multiple_of(group * UNROLL, UNROLL)
        masses = mass_ref[pl.ds(first, UNROLL), :].astype(jnp.float32)
        counts = [
            jnp.broadcast_to(count_ref[pl.ds(first // SUB + h, 1), :], (8, SUB))
            for h in range(UNROLL // SUB)
        ]
        for eight in range(UNROLL // 8):
            z_chain, y_chain = chains[2 * eight], chains[2 * eight + 1]
            base = pl.multiple_of(first + 8 * eight, 8)
            cells = cells_ref[pl.ds(base, 8), :]
            count = jnp.take_along_axis(
                counts[8 * eight // SUB],
                number + 8 * eight % SUB,
                axis=1,
                mode="promise_in_bounds",
            )
            weight = jnp.where(lane < count, masses[8 * eight : 8 * eight + 8], 0.0)
            z_at = ((cells & (SUB - 1)).astype(jnp.float32) - (SUB - 1) / 2) * (2 / SUB)
            y_at = (((cells >> 7) & (SUB - 1)).astype(jnp.float32) - (SUB - 1) / 2) * (2 / SUB)
            chain(z_chain, weight, z_at)
            chain(y_chain, jnp.ones_like(weight), y_at)
            lower_half = (cells >> 14).astype(jnp.float32)
            for pair in range(0, 8, 2):
                left, right = [], []
                for j in (pair, pair + 1):
                    rows = [pl.ds(64 * i + j, 8, stride=8) for i in range(Q // 8)]
                    left.append(split(jnp.concatenate([z_chain[r, :] for r in rows], axis=0)))
                    high, low = split(jnp.concatenate([y_chain[r, :] for r in rows], axis=0))
                    second = lower_half[j : j + 1]
                    first_half = (1.0 - second).astype(jnp.bfloat16)
                    second = second.astype(jnp.bfloat16)
                    right.append(
                        jnp.concatenate(
                            [high * first_half, high * second, low * first_half, low * second],
                            axis=0,
                        )
                    )
                left = jnp.concatenate(
                    [
                        jnp.concatenate([left[0][0], left[0][1], none, none], axis=0),
                        jnp.concatenate([none, none, left[1][0], left[1][1]], axis=0),
                    ],
                    axis=1,
                )
                part = lax.dot_general(
                    left,
                    jnp.concatenate(right, axis=1),
                    (((1,), (1,)), ((), ())),
                    preferred_element_type=jnp.float32,
                )
                for j in range(2):
                    blocks[base + (1 + pair + j)] = (
                        part[64 * j : 64 * j + 32] + part[64 * j + 32 : 64 * j + 64]
                    )
        return carry

    steps = cells_ref.shape[0] // UNROLL
    lax.fori_loop(0, steps // 2, both, 0)
    between()
    lax.fori_loop(steps // 2, steps, step, 0)


def collect(plane, first_ref, second_ref, blocks, tiles):
    upper = lax.broadcasted_iota(jnp.int32, (Q, SUB), 1) >= SUB // 2

    def named(device):
        return blocks[first_ref[plane, device]] + blocks[second_ref[plane, device]]

    for col in range(N_PY):
        for i in range(4):
            even = named(2 * i * N_PY + col)
            odd = named((2 * i + 1) * N_PY + col)
            tile = jnp.where(upper, odd, even)
            tile = tile + pltpu.roll(jnp.where(upper, even, odd), SUB // 2, 1)
            tiles[Q * col : Q * col + Q, SUB * i : SUB * i + SUB] = tile


def z_transform(j, tiles, half, z_ref):
    for n in range(2):
        lanes = slice(256 * n, 256 * n + 256)
        product = 0.0
        for k in range(2):
            depth = slice(256 * k, 256 * k + 256)
            high, low = split(tiles[depth, lanes])
            both = dot(z_ref[:, depth], high)
            product += both[:ROWS] + both[ROWS:] + dot(z_ref[:ROWS, depth], low)
        for c in range(2):
            half[c, MEET * j : MEET * j + 64, lanes] = product[64 * c : 64 * c + 64]
            half[c, MEET * j + 64 : MEET * j + MEET, lanes] = product[128:ROWS]


def y_transform(half, y_ref, stage):
    sides = []
    for c in range(2):
        high, low = split(half[c])
        sides.append(dot(jnp.concatenate([high, low, high], axis=1), y_ref[c]))
    real, imag = sides
    top = lax.broadcasted_iota(jnp.int32, (8, 2 * KY), 0) == 0
    for j in range(HELD):
        a, b = real[MEET * j : MEET * j + MEET], imag[MEET * j : MEET * j + MEET]
        minus = a[:64] - b[:64]
        last = jnp.broadcast_to(a[64:65] - b[65:66], (8, 2 * KY))
        minus = jnp.concatenate([jnp.where(top, last, minus[:8]), minus[8:]], axis=0)
        for c in range(2):
            lanes = slice(KY * c, KY * c + KY)
            stage[j, c, 0:64, :] = (a[:64] + b[:64])[:, lanes]
            stage[j, c, 64:128, :] = minus[:, lanes]


def slot_of(device):
    ahead = device >> 6
    return ahead * (device - 64) + (1 - ahead) * (64 + ((128 - device) & 63))


def mesh_kernel(
    dest_hbm, count_hbm, screen_ref, cells_hbm, mass_hbm, z_hbm, y_hbm, wave_hbm, out_ref,
    dest, count, cells, mass, z_ref, y_ref, wave, most, least, first, second, first_at, second_at,
    blocks, tiles_a, tiles_b, half, stage, get, send, landed,
    load_sems, table_sems, give_sem, get_sem, send_sem, land_sem, *chains,
):
    px, py = lax.axis_index("px"), lax.axis_index("py")
    me = px * N_PY + py
    core = lax.rem(px, 2)
    sibling = px + 1 - 2 * core
    loads = [
        pltpu.make_async_copy(a, b, load_sems.at[i])
        for i, (a, b) in enumerate(
            [
                (dest_hbm, dest),
                (count_hbm, count),
                (cells_hbm, cells),
                (mass_hbm, mass),
                (z_hbm, z_ref),
                (y_hbm, y_ref),
                (wave_hbm.at[pl.ds(me, 1)], wave),
            ]
        )
    ]
    for load in loads[:4]:
        load.start()
    barrier = pltpu.get_barrier_semaphore()

    def greet(k):
        to = (me + k) & (DEVICES - 1)
        pl.semaphore_signal(
            barrier, inc=1, device_id=(to >> 4, to & (N_PY - 1)), device_id_type=MESH
        )

    def greet_some(step, carry):
        for j in range(8):
            greet(7 + 8 * step + j)
        return carry

    for k in range(1, 7):
        greet(k)
    lax.fori_loop(0, 15, greet_some, 0)
    greet(DEVICES - 1)

    def beside(group):
        for j in range(8):
            tile_blocks(group * 8 + j, dest, most, least)

    for load in loads[:4]:
        load.wait()
    tables = [
        pltpu.make_async_copy(first, first_at, table_sems.at[0]),
        pltpu.make_async_copy(second, second_at, table_sems.at[1]),
    ]

    def between():
        tile_table(most, least, first, second)
        for copy in tables + loads[4:]:
            copy.start()

    block_products(count, cells, mass, blocks, chains, beside, between)
    for copy in loads[4:] + tables:
        copy.wait()
    handover = pltpu.make_async_remote_copy(
        src_ref=stage.at[0],
        dst_ref=get,
        send_sem=give_sem,
        recv_sem=get_sem,
        device_id=(sibling, py),
        device_id_type=MESH,
    )

    def batch(b, carry):
        base = HELD * (b * core + (1 - b) * (1 - core))
        tiles = (tiles_a, tiles_b)
        collect(base, first_at, second_at, blocks, tiles[0])
        for j in range(HELD):
            z_transform(j, tiles[j % 2], half, z_ref)
            if j + 1 < HELD:
                collect(base + (j + 1), first_at, second_at, blocks, tiles[(j + 1) % 2])
        y_transform(half, y_ref, stage.at[b])

        @pl.when(b == 0)
        def _():
            pl.semaphore_wait(barrier, DEVICES - 1)
            handover.start()

        return carry

    lax.fori_loop(0, 2, batch, 0)
    handover.wait_recv()
    for j in range(HELD):
        for c in range(2):
            send[pl.ds(HELD * c + j, 128, stride=PARTS), :] = stage[1, j, c] + get[j, c]
    place = pl.multiple_of((core * 64 + (px // 2) * N_PY + py) * PARTS, PARTS)

    def post(k, carry):
        to = (me + k) & (DEVICES - 1)
        pltpu.make_async_remote_copy(
            src_ref=send.at[pl.ds(pl.multiple_of(slot_of(to) * PARTS, PARTS), PARTS)],
            dst_ref=landed.at[pl.ds(place, PARTS)],
            send_sem=send_sem,
            recv_sem=land_sem,
            device_id=(to >> 4, to & (N_PY - 1)),
            device_id_type=MESH,
        ).start()
        return carry

    lax.fori_loop(1, DEVICES, post, 0)
    landed[pl.ds(place, PARTS), :] = send[
        pl.ds(pl.multiple_of(slot_of(me) * PARTS, PARTS), PARTS), :
    ]
    bulk = landed.at[pl.ds(0, (DEVICES - 1) * PARTS)]
    pltpu.make_async_copy(bulk, bulk, land_sem).wait()
    for h in range(2):
        total = jnp.sum(landed[512 * h : 512 * h + 512, :].reshape(64, PARTS, KY), axis=0)
        for j in range(HELD):
            scr = screen_ref[HELD * h + j]
            wave_sq = wave[...]
            green = jnp.where(wave_sq == 0.0, 0.0, -scr / (wave_sq + scr))
            green = green * (1.0 / math.sqrt(NY * NZ))
            for c in range(2):
                row = total[HELD * c + j : HELD * c + j + 1, :]
                out_ref[HELD * h + j, c : c + 1, :] = row * green
    pltpu.make_async_copy(bulk, bulk, send_sem).wait()
    handover.wait_send()


def wave_table():
    z_wave = (2.0 * np.sin(np.pi * (np.arange(KZ) - KZ // 2) / NZ)) ** 2
    y_wave = (2.0 * np.sin(np.pi * (np.arange(KY) - KY // 2) / NY)) ** 2
    return (z_wave[:, None] + y_wave[None, :]).astype(np.float32)


def shards(cell_ids, masses, block_dest, block_count, screen):
    blocks = cell_ids.shape[0]
    f32, bf16, i32 = jnp.float32, jnp.bfloat16, jnp.int32
    dma = pltpu.SemaphoreType.DMA
    modes = pl.pallas_call(
        mesh_kernel,
        out_shape=jax.ShapeDtypeStruct((PL, 2, KY), f32),
        in_specs=[
            pl.BlockSpec(memory_space=pltpu.SMEM if i == 2 else pl.ANY) for i in range(8)
        ],
        out_specs=pl.BlockSpec(memory_space=pltpu.VMEM),
        scratch_shapes=[
            pltpu.VMEM((8, SUB), i32),
            pltpu.VMEM((8, SUB), i32),
            pltpu.VMEM((blocks, SUB), i32),
            pltpu.VMEM((blocks, SUB), bf16),
            pltpu.VMEM((2 * ROWS, SPAN), bf16),
            pltpu.VMEM((2, 3 * SPAN, 2 * KY), bf16),
            pltpu.VMEM((1, KY), f32),
            pltpu.VMEM((16, PL, SUB), i32),
            pltpu.VMEM((16, PL, SUB), i32),
            pltpu.VMEM((8, SUB), i32),
            pltpu.VMEM((8, SUB), i32),
            pltpu.SMEM((8, SUB), i32),
            pltpu.SMEM((8, SUB), i32),
            pltpu.VMEM((blocks + 1, Q, SUB), f32),
            pltpu.VMEM((SPAN, SPAN), f32),
            pltpu.VMEM((SPAN, SPAN), f32),
            pltpu.VMEM((2, HELD * MEET, SPAN), f32),
            pltpu.VMEM((2, HELD, 2, KZ, KY), f32),
            pltpu.VMEM((HELD, 2, KZ, KY), f32),
            pltpu.VMEM((DEVICES * PARTS + PARTS, KY), f32),
            pltpu.VMEM((DEVICES * PARTS, KY), f32),
            dma((7,)),
            dma((2,)),
            dma,
            dma,
            dma,
            dma,
        ]
        + [pltpu.VMEM((Q * 8 + 8, SUB), f32)] * (UNROLL // 4),
        compiler_params=pltpu.CompilerParams(
            collective_id=0, has_side_effects=True, vmem_limit_bytes=60 << 20
        ),
    )(
        block_dest.reshape(8, SUB),
        block_count.reshape(8, SUB),
        screen,
        cell_ids,
        masses,
        jnp.asarray(z_table()),
        jnp.asarray(y_table()),
        jnp.asarray(wave_table()),
    )
    return jnp.swapaxes(modes, 1, 2)


def solution(mesh):
    return jax.shard_map(
        shards,
        mesh=mesh,
        in_specs=(
            P(("px", "py"), None),
            P(("px", "py"), None),
            P(("px", "py"), None),
            P(("px", "py")),
            P(),
        ),
        out_specs=P(None, None, ("px", "py")),
        check_vma=False,
    )
```
